256 devices in a mesh: rows: 8 (over x, core), cols: 32 (over y, z).
Axes of the slice: x: 4, y: 4, z: 8, core: 2. Of those that a mesh axis runs over, the one named last changes fastest.
Arguments:
- features: bfloat16 [256, 4096, 1536], P('rows', 'cols'), may hold values from -6 to 6
- projection: bfloat16 [1536, 128], replicated, may hold values from -0.4375 to 0.4375
- prev_dist: float32 [256, 4096], P('rows', 'cols'), may hold values from 0.5 to 3
- valid: int32 [256, 4096], P('rows', 'cols'), may hold values 0 or 1
- pick_owner: int32 [512], replicated, may hold values from 0 to 255, as said below
- pick_slot: int32 [512], replicated, may hold values from 0 to 4095, as said below
Outputs:
- min_dist: float32 [256, 4096], P('rows', 'cols')
The draws below stay inside these ranges and needn't reach their ends.
Inputs may be any that keep to these rules, and one draw needn't show every extreme that they name: `pick_owner`: no two picks name the same patch; picks fall on devices at random. `pick_slot`: see pick_owner.
All inputs are finite; a program needn't handle non-finite values. No bound on the sum of `valid` on one device may be relied on, other than what follows from the above.
Results may differ from the reference program's by a relative error of at most 0.0003.
Values may be sent and summed in bfloat16 or wider, within the bound.
A program may use at most 128 MiB of HBM per device.

```python
import jax
import jax.numpy as jnp
from jax import lax

C = 1536
D_PROJ = 128
K = 512
H_DEV = 32
W_DEV = 128
NH = 256
NW = 4096
N_COLS = 32
DEVICES = 256


def pick_pairs(key):
    inner_key = jax.random.fold_in(key, 7)
    order_key = jax.random.fold_in(key, 11)
    per_device = H_DEV * W_DEV
    total = per_device * DEVICES
    middle = jax.random.permutation(inner_key, total - 2)[:K - 2].astype(jnp.int32) + 1
    ends = jnp.array([0, total - 1], dtype=jnp.int32)
    chosen = jnp.concatenate([ends, middle])
    chosen = jax.random.permutation(order_key, chosen)
    return (chosen // per_device, chosen % per_device)


def draw_pick_owner(key, part):
    return pick_pairs(key)[0]


def draw_pick_slot(key, part):
    return pick_pairs(key)[1]


def set_ends(values, stream_key, least, top_value):
    index_at = [jax.random.randint(jax.random.fold_in(stream_key, axis), (), 0, length) for axis, length in enumerate(values.shape)]
    longest = values.shape.index(max(values.shape))
    beside = index_at[:longest] + [(index_at[longest] + 1) % values.shape[longest]] + index_at[longest + 1:]
    return values.at[tuple(index_at)].set(least).at[tuple(beside)].set(top_value)


def steps_of(own_key, extent, shards, smallest, high):
    def one(position, blocks):
        steps = jax.random.uniform(jax.random.fold_in(jax.random.fold_in(own_key, 6), position), (blocks,), jnp.float32, smallest / len(shards), high / len(shards))
        return jnp.repeat(jnp.exp(steps), extent[position] // blocks).reshape((-1,) + (1,) * (len(extent) - position - 1))

    loudness = one(*shards[0])
    for cut in shards[1:]:
        loudness = loudness * one(*cut)
    return loudness


def scatter_about(rng, extent, deviation, most, split=(), kind=jnp.bfloat16):
    factor_of = steps_of(rng, extent, split, -0.22, 0.18) if split else 1.0
    drawn = jax.random.normal(rng, extent, jnp.float32) * deviation * factor_of
    return jnp.minimum(jnp.maximum(drawn, -most), most).astype(kind)


def setup_inputs(seed: int = 0) -> dict:
    keys = jax.random.split(jax.random.key(seed), 7)
    features = scatter_about(keys[0], (NH, NW, C), 1.0, 6.0, ((0, 8), (1, 32)))
    projection = scatter_about(keys[1], (C, D_PROJ), (C // 9) ** -0.5, 0.4375)
    prev_dist = jnp.clip(0.5 + 2.5 * jax.random.uniform(keys[2], (NH, NW), jnp.float32) ** steps_of(keys[2], (NH, NW), ((0, 8), (1, 32)), -0.2, 0.2), 0.5, 3.0)
    valid = set_ends((jax.random.randint(keys[3], (NH, NW), 0, 4) < 3).astype(jnp.int32), jax.random.fold_in(keys[3], 1), 0, 1)
    pick_owner = draw_pick_owner(jax.random.fold_in(keys[6], 71), 0)
    pick_slot = draw_pick_slot(jax.random.fold_in(keys[6], 71), 0)
    return dict(features=features, projection=projection, prev_dist=prev_dist, valid=valid, pick_owner=pick_owner, pick_slot=pick_slot)


def reference(features, projection, prev_dist, valid, pick_owner, pick_slot):
    grid_rows, grid_cols, channels = features.shape
    proj_full = projection.astype(jnp.float32)
    pick_row = (pick_owner // N_COLS) * H_DEV + pick_slot // W_DEV
    pick_col = (pick_owner % N_COLS) * W_DEV + pick_slot % W_DEV
    accum_sum = jnp.zeros((pick_owner.shape[0], channels), jnp.float32)
    for row_off in (-1, 0, 1):
        for col_off in (-1, 0, 1):
            row_at = pick_row + row_off
            col_at = pick_col + col_off
            inside = (row_at >= 0) & (row_at < grid_rows) & (col_at >= 0) & (col_at < grid_cols)
            values = features[jnp.clip(row_at, 0, grid_rows - 1), jnp.clip(col_at, 0, grid_cols - 1)].astype(jnp.float32)
            accum_sum = accum_sum + jnp.where(inside[:, None], values, jnp.float32(0.0))
    pick_pooled = accum_sum / 9.0
    pick_rows = jnp.dot(pick_pooled, proj_full, precision=lax.Precision.HIGHEST)
    pick_sq = jnp.sum(pick_rows * pick_rows, axis=1)

    def one_row(row_index):
        band_sum = jnp.zeros((grid_cols, channels), jnp.float32)
        for row_off in (-1, 0, 1):
            row_at = row_index + row_off
            inside = (row_at >= 0) & (row_at < grid_rows)
            picked = lax.dynamic_index_in_dim(features, jnp.clip(row_at, 0, grid_rows - 1).astype(jnp.int32), 0, keepdims=False)
            band_sum = band_sum + jnp.where(inside, picked.astype(jnp.float32), jnp.float32(0.0))
        widened = jnp.pad(band_sum, ((1, 1), (0, 0)))
        pooled = (widened[:-2] + widened[1:-1] + widened[2:]) / 9.0
        projected = jnp.dot(pooled, proj_full, precision=lax.Precision.HIGHEST)
        inner_prod = jnp.dot(projected, pick_rows.T, precision=lax.Precision.HIGHEST)
        own_sq = jnp.sum(projected * projected, axis=1)
        scaled_gap = (own_sq[:, None] + pick_sq[None, :] - 2.0 * inner_prod) / D_PROJ
        nearest = jnp.min(scaled_gap, axis=1)
        prev_row = lax.dynamic_index_in_dim(prev_dist, row_index, 0, keepdims=False)
        valid_row = lax.dynamic_index_in_dim(valid, row_index, 0, keepdims=False)
        return jnp.where(valid_row == 1, jnp.minimum(prev_row, nearest), jnp.float32(0.0))

    return lax.map(one_row, jnp.arange(grid_rows, dtype=jnp.int32))
```

```python
import jax
import jax.numpy as jnp
from jax import lax
from jax.experimental import pallas as pl
from jax.experimental.pallas import tpu as pltpu
from jax.sharding import PartitionSpec as P

D_PROJ = 128
MESH = pl.DeviceIdType.MESH
F32, BF16 = jnp.float32, jnp.bfloat16

ROWS, COLS, CHANNELS, PICKS = 32, 128, 1536, 512
SLOTS = 8
CHUNK = 4
CHUNKS = ROWS // CHUNK
LEFT = (ROWS + 2) * COLS
RIGHT = LEFT + 48
TABLE = RIGHT + 48


def padded_2(block, sides, width):
    for axis, dim in sides:
        count = lax.axis_size(axis)
        forward = [(i, i + 1) for i in range(count - 1)]
        backward = [(target, source) for source, target in forward]
        low = lax.ppermute(
            lax.slice_in_dim(block, block.shape[dim] - width, None, axis=dim), axis, forward
        )
        high = lax.ppermute(lax.slice_in_dim(block, 0, width, axis=dim), axis, backward)
        block = jnp.concatenate([low, block, high], axis=dim)
    return block


def window_sum(padded, rows_dev, cols_dev):
    total = jnp.zeros((rows_dev, cols_dev, padded.shape[2]), jnp.float32)
    for row_off in range(3):
        for col_off in range(3):
            total = total + padded[
                row_off : row_off + rows_dev, col_off : col_off + cols_dev
            ].astype(jnp.float32)
    return total / 9.0


def any_picks(features, projection, prev_dist, valid, pick_owner, pick_slot):
    rows_dev, cols_dev, channels = features.shape
    proj_full = projection.astype(jnp.float32)
    own_index = lax.axis_index("rows") * lax.axis_size("cols") + lax.axis_index("cols")
    owned = pick_owner == own_index
    padded = padded_2(features, (("rows", 0), ("cols", 1)), 1)
    pooled = window_sum(padded, rows_dev, cols_dev).reshape(rows_dev * cols_dev, channels)
    projected = jnp.dot(pooled, proj_full, precision=lax.Precision.HIGHEST)
    local_rows = jnp.where(owned[:, None], projected[pick_slot], jnp.float32(0.0))
    pick_rows = lax.psum(local_rows, ("rows", "cols"))
    pick_sq = jnp.sum(pick_rows * pick_rows, axis=1)
    own_sq = jnp.sum(projected * projected, axis=1)
    inner_prod = jnp.dot(projected, pick_rows.T, precision=lax.Precision.HIGHEST)
    scaled_gap = (own_sq[:, None] + pick_sq[None, :] - 2.0 * inner_prod) / D_PROJ
    nearest = jnp.min(scaled_gap, axis=1).reshape(rows_dev, cols_dev)
    return jnp.where(valid == 1, jnp.minimum(prev_dist, nearest), jnp.float32(0.0))


def iota(shape, dim):
    return lax.broadcasted_iota(jnp.int32, shape, dim)


def dot(a, b):
    return jnp.dot(a, b, preferred_element_type=F32)


def touches(pick_row, pick_col, row0, col0):
    down, across = pick_row - row0, pick_col - col0
    return (down >= -1) & (down <= ROWS) & (across >= -1) & (across <= COLS)


def kernel(
    feat_hbm, proj_ref, prev_ref, valid_ref, owner_ref, slot_ref, out_ref, most_ref,
    feat, table, hsum, edge, mine, line, plane, part, other, onehot,
    rhs, lhs, own_sq, best, from_up, from_down, from_left, from_right, corner, side,
    load_sem, send_sem, recv_sem, halo_send, halo_recv,
):
    r, c = lax.axis_index("rows"), lax.axis_index("cols")
    x, core = r // 2, r % 2
    y, z = c // 8, c % 8
    up, down = lax.rem(r + 7, 8), lax.rem(r + 1, 8)
    left, right = lax.rem(c + 31, 32), lax.rem(c + 1, 32)

    def on_line(step):
        return (r, y * 8 + lax.rem(z + step, 8))

    def on_plane(step):
        return (lax.rem(x + step // 4, 4) * 2 + core, lax.rem(y + step % 4, 4) * 8 + z)

    loads = [
        pltpu.make_async_copy(
            feat_hbm.at[pl.ds(i * CHUNK, CHUNK)], feat.at[pl.ds(i * CHUNK, CHUNK)], load_sem.at[i]
        )
        for i in range(CHUNKS)
    ]
    for load in loads:
        load.start()

    barrier = pltpu.get_barrier_semaphore()

    def greet(device):
        pl.semaphore_signal(barrier, inc=1, device_id=device, device_id_type=MESH)

    def greet_line(step, _):
        greet(on_line(step))
        return 0

    def greet_plane(step, _):
        greet(on_plane(step))
        return 0

    lax.fori_loop(1, 8, greet_line, 0)
    lax.fori_loop(1, 16, greet_plane, 0)
    around = [(up, c), (down, c), (r, left), (r, right)]
    around += [(up, left), (up, right), (down, left), (down, right)]
    for device in around:
        greet(device)

    owner, slot = owner_ref[...], slot_ref[...]
    pick_row = (owner >> 5) * ROWS + (slot >> 7)
    pick_col = (owner & 31) * COLS + (slot & 127)
    here = jnp.broadcast_to(touches(pick_row, pick_col, r * ROWS, c * COLS), (8, PICKS))
    before = (iota((PICKS, PICKS), 0) < iota((PICKS, PICKS), 1)).astype(F32).astype(BF16)
    rank = dot(here.astype(F32).astype(BF16), before)
    tile_row, tile_col = pick_row - r * ROWS, pick_col - c * COLS
    end = jnp.where(tile_row == -1, 32, jnp.where(tile_row == ROWS, 40, tile_row))
    place = (tile_row + 1) * COLS + tile_col
    place = jnp.where(tile_col == -1, LEFT + end, place)
    place = jnp.where(tile_col == COLS, RIGHT + end, place)
    chosen = here & (rank == iota((8, PICKS), 0).astype(F32))
    places = jnp.sum(
        jnp.where(chosen, jnp.broadcast_to(place, (8, PICKS)).astype(F32), 0.0), axis=1, keepdims=True
    ).astype(jnp.int32)
    places = jnp.clip(places, 0, TABLE - 1)
    filled = jnp.sum(chosen.astype(F32), axis=1, keepdims=True)

    zero_row = jnp.zeros((1, COLS, D_PROJ), F32)
    hsum[0:2] = jnp.zeros((2, COLS, D_PROJ), F32)
    hsum[ROWS + 2 : ROWS + 4] = jnp.zeros((2, COLS, D_PROJ), F32)
    edge[...] = jnp.zeros_like(edge)
    proj = proj_ref[...]
    sub = iota((COLS, D_PROJ), 0)

    for i in range(CHUNKS):
        loads[i].wait()
        block = feat[i * CHUNK : (i + 1) * CHUNK].reshape(CHUNK * COLS, CHANNELS)
        raw = dot(block, proj).reshape(CHUNK, COLS, D_PROJ)
        for k in range(CHUNK):
            one = raw[k]
            row = i * CHUNK + k
            before_it = jnp.where(sub == 0, 0.0, pltpu.roll(one, 1, 0))
            after_it = jnp.where(sub == COLS - 1, 0.0, pltpu.roll(one, COLS - 1, 0))
            hsum[row + 2] = one + before_it + after_it
            edge[0, row + 8 : row + 9] = one[0:1]
            edge[1, row + 8 : row + 9] = one[COLS - 1 : COLS]
        for k in range(CHUNK):
            row = i * CHUNK + k - 1
            table[(row + 1) * COLS : (row + 2) * COLS] = hsum[row + 1] + hsum[row + 2] + hsum[row + 3]
    for row in (ROWS - 1, ROWS):
        table[(row + 1) * COLS : (row + 2) * COLS] = hsum[row + 1] + hsum[row + 2] + hsum[row + 3]
    for s, base in enumerate((LEFT, RIGHT)):
        table[base : base + 32] = edge[s, 7:39] + edge[s, 8:40] + edge[s, 9:41]
        table[base + 32 : base + 40] = jnp.broadcast_to(edge[s, 8:9], (8, D_PROJ))
        table[base + 40 : base + 48] = jnp.broadcast_to(edge[s, 39:40], (8, D_PROJ))

    for j in range(SLOTS):
        mine[j : j + 1] = table[pl.ds(places[j, 0], 1), :]
    mine[...] = jnp.where(filled > 0.0, mine[...], 0.0)
    line[z] = mine[...]

    pl.semaphore_wait(barrier, 30)

    def send_line(step, _):
        pltpu.make_async_remote_copy(
            mine, line.at[z], send_sem.at[0], recv_sem.at[0],
            device_id=on_line(step), device_id_type=MESH,
        ).start()
        return 0

    lax.fori_loop(1, 8, send_line, 0)

    halos = [
        (table.at[pl.ds(0, COLS)], from_down, (up, c)),
        (table.at[pl.ds((ROWS + 1) * COLS, COLS)], from_up, (down, c)),
        (table.at[pl.ds(LEFT, 32)], from_right, (r, left)),
        (table.at[pl.ds(RIGHT, 32)], from_left, (r, right)),
        (table.at[pl.ds(LEFT + 32, 8)], corner.at[3], (up, left)),
        (table.at[pl.ds(RIGHT + 32, 8)], corner.at[2], (up, right)),
        (table.at[pl.ds(LEFT + 40, 8)], corner.at[1], (down, left)),
        (table.at[pl.ds(RIGHT + 40, 8)], corner.at[0], (down, right)),
    ]
    halo_copies = []
    for n, (source, target, device) in enumerate(halos):
        copy = pltpu.make_async_remote_copy(
            source, target, halo_send.at[n], halo_recv.at[n], device_id=device, device_id_type=MESH
        )
        copy.start()
        halo_copies.append(copy)

    grid = jnp.concatenate(
        [jnp.broadcast_to(pick_row, (4, PICKS)), jnp.broadcast_to(pick_col, (4, PICKS))], axis=0
    ).astype(F32)
    grid = grid.T
    rows_k, cols_k = grid[:, 0:1], grid[:, 4:5]
    d = iota((1, 128), 1)
    row0 = (((d >> 5) * 2) * ROWS).astype(F32)
    col0 = ((((d >> 3) & 3) * 8 + (d & 7)) * COLS).astype(F32)
    most = jnp.zeros((1, 128), F32)
    for half in range(2):
        over = touches(rows_k, cols_k, row0 + half * ROWS, col0).astype(F32)
        most = jnp.maximum(most, jnp.sum(over, axis=0, keepdims=True))
    most_ref[...] = jnp.broadcast_to(jnp.max(most, axis=1, keepdims=True), (8, 128))
    over = touches(rows_k, cols_k, row0 + (core * ROWS).astype(F32), col0)
    earlier = (iota((PICKS, PICKS), 1) < iota((PICKS, PICKS), 0)).astype(F32).astype(BF16)
    ranks = dot(earlier, over.astype(F32).astype(BF16))
    ranks = jnp.where(over, jnp.minimum(ranks, 64.0), 100.0).astype(BF16)
    spread = ((iota((128, 1024), 1) >> 3) == iota((128, 1024), 0)).astype(F32).astype(BF16)
    onehot[...] = (
        (dot(ranks, spread) == (iota((PICKS, 1024), 1) & 7).astype(F32)).astype(F32).astype(BF16)
    )

    pltpu.make_async_copy(line.at[pl.ds(0, 7)], line.at[pl.ds(0, 7)], recv_sem.at[0]).wait()
    me = x * 4 + y

    def send_plane(step, _):
        pltpu.make_async_remote_copy(
            line, plane.at[me], send_sem.at[1], recv_sem.at[1],
            device_id=on_plane(step), device_id_type=MESH,
        ).start()
        return 0

    lax.fori_loop(1, 16, send_plane, 0)
    plane[me] = line[...]

    for copy in halo_copies:
        copy.wait_recv()
    has_up, has_down = (r > 0).astype(F32), (r < 7).astype(F32)
    has_left, has_right = (c > 0).astype(F32), (c < 31).astype(F32)
    pooled = jnp.concatenate(
        [corner[n, 0:1] for n in range(4)], axis=0
    )
    side[0] = from_left[...] * has_left
    side[1] = from_right[...] * has_right
    side[0, 0:1] += pooled[0:1] * (has_up * has_left)
    side[1, 0:1] += pooled[1:2] * (has_up * has_right)
    side[0, 31:32] += pooled[2:3] * (has_down * has_left)
    side[1, 31:32] += pooled[3:4] * (has_down * has_right)
    hsum[0] = from_up[...] * has_up
    hsum[1] = from_down[...] * has_down

    def lay_out(i, _):
        at = pl.multiple_of(i * COLS, COLS)
        one = table[pl.ds(at + COLS, COLS), :]
        one += jnp.where(sub == 0, side[0, pl.ds(i, 1), :], 0.0)
        one += jnp.where(sub == COLS - 1, side[1, pl.ds(i, 1), :], 0.0)
        one += jnp.where(i == 0, hsum[0], 0.0) + jnp.where(i == ROWS - 1, hsum[1], 0.0)
        flipped = one.T
        own_sq[pl.ds(i, 1), :] = jnp.sum(flipped * flipped, axis=0, keepdims=True)
        high = flipped.astype(BF16)
        low = (flipped - high.astype(F32)).astype(BF16)
        rhs[0:128, pl.ds(at, COLS)] = high
        rhs[128:256, pl.ds(at, COLS)] = low
        rhs[256:384, pl.ds(at, COLS)] = high
        rhs[384:512, pl.ds(at, COLS)] = jnp.ones((128, COLS), BF16)
        return 0

    lax.fori_loop(0, ROWS, lay_out, 0)

    pltpu.make_async_copy(plane.at[pl.ds(0, 15)], plane.at[pl.ds(0, 15)], recv_sem.at[1]).wait()
    got = plane[...].reshape(1024, D_PROJ)
    high = got.astype(BF16)
    low = (got - high.astype(F32)).astype(BF16)
    both = dot(onehot[...], jnp.concatenate([high, low], axis=1))
    part[...] = both[:, :D_PROJ] + both[:, D_PROJ:]
    swap = pltpu.make_async_remote_copy(
        part, other, send_sem.at[2], recv_sem.at[2],
        device_id=(x * 2 + 1 - core, c), device_id_type=MESH,
    )
    swap.start()
    swap.wait_recv()

    picks = part[...] + other[...]
    high = picks.astype(BF16)
    lhs[:, 0:128] = high
    lhs[:, 128:256] = high
    lhs[:, 256:384] = (picks - high.astype(F32)).astype(BF16)
    half_sq = jnp.sum(picks * picks, axis=1, keepdims=True) * -0.5
    first = half_sq.astype(BF16).astype(F32)
    second = (half_sq - first).astype(BF16).astype(F32)
    third = half_sq - first - second
    lane = iota((PICKS, 128), 1)
    tail = jnp.where(lane == 0, first, jnp.where(lane == 1, second, jnp.where(lane == 2, third, 0.0)))
    lhs[:, 384:512] = tail.astype(BF16)

    def nearest(i, _):
        at = pl.multiple_of(i * 256, 256)
        score = jnp.max(dot(lhs[...], rhs[:, pl.ds(at, 256)]), axis=0, keepdims=True)
        best[pl.ds(2 * i, 1), :] = score[:, :128]
        best[pl.ds(2 * i + 1, 1), :] = score[:, 128:]
        return 0

    lax.fori_loop(0, ROWS // 2, nearest, 0)
    gap = (own_sq[...] - 2.0 * best[...]) * (1.0 / (81.0 * D_PROJ))
    out_ref[...] = jnp.where(valid_ref[...] == 1, jnp.minimum(prev_ref[...], gap), 0.0)

    pltpu.make_async_copy(line.at[pl.ds(0, 7)], line.at[pl.ds(0, 7)], send_sem.at[0]).wait()
    pltpu.make_async_copy(plane.at[pl.ds(0, 15)], plane.at[pl.ds(0, 15)], send_sem.at[1]).wait()
    swap.wait_send()
    for copy in halo_copies:
        copy.wait_send()


def shards(features, projection, prev_dist, valid, pick_owner, pick_slot):
    vmem = pl.BlockSpec(memory_space=pltpu.VMEM)
    result, most = pl.pallas_call(
        kernel,
        out_shape=(
            jax.ShapeDtypeStruct((ROWS, COLS), F32),
            jax.ShapeDtypeStruct((8, 128), F32),
        ),
        in_specs=[pl.BlockSpec(memory_space=pltpu.HBM)] + [vmem] * 5,
        out_specs=(vmem, vmem),
        scratch_shapes=[
            pltpu.VMEM((ROWS, COLS, CHANNELS), BF16),
            pltpu.VMEM((TABLE, D_PROJ), F32),
            pltpu.VMEM((ROWS + 4, COLS, D_PROJ), F32),
            pltpu.VMEM((2, 48, D_PROJ), F32),
            pltpu.VMEM((SLOTS, D_PROJ), F32),
            pltpu.VMEM((8, SLOTS, D_PROJ), F32),
            pltpu.VMEM((16, 8, SLOTS, D_PROJ), F32),
            pltpu.VMEM((PICKS, D_PROJ), F32),
            pltpu.VMEM((PICKS, D_PROJ), F32),
            pltpu.VMEM((PICKS, 1024), BF16),
            pltpu.VMEM((512, ROWS * COLS), BF16),
            pltpu.VMEM((PICKS, 512), BF16),
            pltpu.VMEM((ROWS, COLS), F32),
            pltpu.VMEM((ROWS, COLS), F32),
            pltpu.VMEM((COLS, D_PROJ), F32),
            pltpu.VMEM((COLS, D_PROJ), F32),
            pltpu.VMEM((ROWS, D_PROJ), F32),
            pltpu.VMEM((ROWS, D_PROJ), F32),
            pltpu.VMEM((4, 8, D_PROJ), F32),
            pltpu.VMEM((2, ROWS, D_PROJ), F32),
            pltpu.SemaphoreType.DMA((CHUNKS,)),
            pltpu.SemaphoreType.DMA((3,)),
            pltpu.SemaphoreType.DMA((3,)),
            pltpu.SemaphoreType.DMA((8,)),
            pltpu.SemaphoreType.DMA((8,)),
        ],
        compiler_params=pltpu.CompilerParams(
            collective_id=0, has_side_effects=True, vmem_limit_bytes=56 << 20
        ),
        name="coreset",
    )(
        features, projection, prev_dist, valid,
        pick_owner.reshape(1, PICKS), pick_slot.reshape(1, PICKS),
    )
    return lax.cond(
        most[0, 0] > SLOTS,
        any_picks,
        lambda *_: result,
        features, projection, prev_dist, valid, pick_owner, pick_slot,
    )


def solution(mesh):
    return jax.shard_map(
        shards,
        mesh=mesh,
        in_specs=(P("rows", "cols", None), P(), P("rows", "cols"), P("rows", "cols"), P(), P()),
        out_specs=P("rows", "cols"),
        check_vma=False,
    )
```

```python
import jax
import jax.numpy as jnp
from jax import lax
from jax.experimental import pallas as pl
from jax.experimental.pallas import tpu as pltpu
from jax.sharding import PartitionSpec as P

D_PROJ = 128
MESH = pl.DeviceIdType.MESH
F32, BF16 = jnp.float32, jnp.bfloat16

ROWS, COLS, CHANNELS, PICKS = 32, 128, 1536, 512
SLOTS = 8
CHUNK = 4
CHUNKS = ROWS // CHUNK
WIDE = COLS + 16
TABLE = (ROWS + 4) * WIDE


def padded_2(block, sides, width):
    for axis, dim in sides:
        count = lax.axis_size(axis)
        forward = [(i, i + 1) for i in range(count - 1)]
        backward = [(target, source) for source, target in forward]
        low = lax.ppermute(
            lax.slice_in_dim(block, block.shape[dim] - width, None, axis=dim), axis, forward
        )
        high = lax.ppermute(lax.slice_in_dim(block, 0, width, axis=dim), axis, backward)
        block = jnp.concatenate([low, block, high], axis=dim)
    return block


def window_sum(padded, rows_dev, cols_dev):
    total = jnp.zeros((rows_dev, cols_dev, padded.shape[2]), jnp.float32)
    for row_off in range(3):
        for col_off in range(3):
            total = total + padded[
                row_off : row_off + rows_dev, col_off : col_off + cols_dev
            ].astype(jnp.float32)
    return total / 9.0


def any_picks(features, projection, prev_dist, valid, pick_owner, pick_slot):
    rows_dev, cols_dev, channels = features.shape
    proj_full = projection.astype(jnp.float32)
    own_index = lax.axis_index("rows") * lax.axis_size("cols") + lax.axis_index("cols")
    owned = pick_owner == own_index
    padded = padded_2(features, (("rows", 0), ("cols", 1)), 1)
    pooled = window_sum(padded, rows_dev, cols_dev).reshape(rows_dev * cols_dev, channels)
    projected = jnp.dot(pooled, proj_full, precision=lax.Precision.HIGHEST)
    local_rows = jnp.where(owned[:, None], projected[pick_slot], jnp.float32(0.0))
    pick_rows = local_rows
    for axis in ("rows", "cols"):
        count, step = lax.axis_size(axis), 1
        while step < count:
            swap = [(i, i ^ step) for i in range(count)]
            pick_rows = pick_rows + lax.ppermute(pick_rows, axis, swap)
            step *= 2
    pick_sq = jnp.sum(pick_rows * pick_rows, axis=1)
    own_sq = jnp.sum(projected * projected, axis=1)
    inner_prod = jnp.dot(projected, pick_rows.T, precision=lax.Precision.HIGHEST)
    scaled_gap = (own_sq[:, None] + pick_sq[None, :] - 2.0 * inner_prod) / D_PROJ
    nearest = jnp.min(scaled_gap, axis=1).reshape(rows_dev, cols_dev)
    return jnp.where(valid == 1, jnp.minimum(prev_dist, nearest), jnp.float32(0.0))


def iota(shape, dim):
    return lax.broadcasted_iota(jnp.int32, shape, dim)


def dot(a, b):
    return jnp.dot(a, b, preferred_element_type=F32)


def touches(pick_row, pick_col, row0, col0):
    down, across = pick_row - row0, pick_col - col0
    return (down >= -1) & (down <= ROWS) & (across >= -1) & (across <= COLS)


def kernel(
    feat_hbm, proj_ref, prev_ref, valid_ref, owner_ref, slot_ref, out_ref, most_ref,
    feat, raw, band, pooled, hrow, edge, ends, mine, line, plane, part, other, onehot,
    rhs, lhs, own_sq, best, from_up, from_down, from_left, from_right, corner, side,
    load_sem, send_sem, recv_sem, halo_send, halo_recv,
):
    r, c = lax.axis_index("rows"), lax.axis_index("cols")
    x, core = r // 2, r % 2
    y, z = c // 8, c % 8
    up, down = lax.rem(r + 7, 8), lax.rem(r + 1, 8)
    left, right = lax.rem(c + 31, 32), lax.rem(c + 1, 32)

    def on_line(step):
        return (r, y * 8 + lax.rem(z + step, 8))

    def on_plane(step):
        return (lax.rem(x + step // 4, 4) * 2 + core, lax.rem(y + step % 4, 4) * 8 + z)

    loads = [
        pltpu.make_async_copy(
            feat_hbm.at[pl.ds(i * CHUNK, CHUNK)], feat.at[pl.ds(i * CHUNK, CHUNK)], load_sem.at[i]
        )
        for i in range(CHUNKS)
    ]
    for load in loads:
        load.start()

    barrier = pltpu.get_barrier_semaphore()

    def greet(device):
        pl.semaphore_signal(barrier, inc=1, device_id=device, device_id_type=MESH)

    def greet_line(step, _):
        greet(on_line(step))
        return 0

    def greet_plane(step, _):
        greet(on_plane(step))
        return 0

    lax.fori_loop(1, 8, greet_line, 0)
    lax.fori_loop(1, 16, greet_plane, 0)
    around = [(up, c), (down, c), (r, left), (r, right)]
    around += [(up, left), (up, right), (down, left), (down, right)]
    for device in around:
        greet(device)

    owner, slot = owner_ref[...], slot_ref[...]
    pick_row = (owner >> 5) * ROWS + (slot >> 7)
    pick_col = (owner & 31) * COLS + (slot & 127)
    here = jnp.broadcast_to(touches(pick_row, pick_col, r * ROWS, c * COLS), (8, PICKS))
    before = (iota((PICKS, PICKS), 0) < iota((PICKS, PICKS), 1)).astype(F32).astype(BF16)
    rank = dot(here.astype(F32).astype(BF16), before)
    tile_row, tile_col = pick_row - r * ROWS, pick_col - c * COLS
    place = (tile_row + 2) * WIDE + tile_col + 8
    chosen = here & (rank == iota((8, PICKS), 0).astype(F32))
    places = jnp.sum(
        jnp.where(chosen, jnp.broadcast_to(place, (8, PICKS)).astype(F32), 0.0), axis=1, keepdims=True
    ).astype(jnp.int32)
    places = jnp.clip(places, WIDE + 1, TABLE - WIDE - 2)
    filled = jnp.sum(chosen.astype(F32), axis=1, keepdims=True)

    raw[0 : 2 * WIDE] = jnp.zeros((2 * WIDE, D_PROJ), F32)
    raw[TABLE - 2 * WIDE :] = jnp.zeros((2 * WIDE, D_PROJ), F32)
    edge[...] = jnp.zeros_like(edge)
    proj = proj_ref[...]
    margin = jnp.zeros((8, D_PROJ), F32)
    for i in range(CHUNKS):
        loads[i].wait()
        block = feat[i * CHUNK : (i + 1) * CHUNK].reshape(CHUNK * COLS, CHANNELS)
        done = dot(block, proj)
        for k in range(CHUNK):
            row = i * CHUNK + k
            one = done[k * COLS : (k + 1) * COLS]
            at = (row + 2) * WIDE
            raw[at : at + 8] = margin
            raw[at + 8 : at + 8 + COLS] = one
            raw[at + 8 + COLS : at + WIDE] = margin
            edge[0, row + 8 : row + 9] = one[0:1]
            edge[1, row + 8 : row + 9] = one[COLS - 1 :]

    for j in range(SLOTS):
        place = places[j, 0]
        near = raw[pl.ds(place - WIDE - 1, 3), :] + raw[pl.ds(place - 1, 3), :]
        near += raw[pl.ds(place + WIDE - 1, 3), :]
        mine[j : j + 1] = near[0:1] + near[1:2] + near[2:3]
    mine[...] = jnp.where(filled > 0.0, mine[...], 0.0)
    line[z] = mine[...]

    pl.semaphore_wait(barrier, 30)

    def send_line(step, _):
        pltpu.make_async_remote_copy(
            mine, line.at[z], send_sem.at[0], recv_sem.at[0],
            device_id=on_line(step), device_id_type=MESH,
        ).start()
        return 0

    lax.fori_loop(1, 8, send_line, 0)

    for n, at in enumerate((2 * WIDE, (ROWS + 1) * WIDE)):
        hrow[n] = raw[at + 7 : at + 7 + COLS] + raw[at + 8 : at + 8 + COLS] + raw[at + 9 : at + 9 + COLS]
    for n in range(2):
        ends[n, 0:32] = edge[n, 7:39] + edge[n, 8:40] + edge[n, 9:41]
        ends[n, 32:40] = jnp.broadcast_to(edge[n, 8:9], (8, D_PROJ))
        ends[n, 40:48] = jnp.broadcast_to(edge[n, 39:40], (8, D_PROJ))
    halos = [
        (hrow.at[0], from_down, (up, c)),
        (hrow.at[1], from_up, (down, c)),
        (ends.at[0, pl.ds(0, 32)], from_right, (r, left)),
        (ends.at[1, pl.ds(0, 32)], from_left, (r, right)),
        (ends.at[0, pl.ds(32, 8)], corner.at[3], (up, left)),
        (ends.at[1, pl.ds(32, 8)], corner.at[2], (up, right)),
        (ends.at[0, pl.ds(40, 8)], corner.at[1], (down, left)),
        (ends.at[1, pl.ds(40, 8)], corner.at[0], (down, right)),
    ]
    halo_copies = []
    for n, (source, target, device) in enumerate(halos):
        copy = pltpu.make_async_remote_copy(
            source, target, halo_send.at[n], halo_recv.at[n], device_id=device, device_id_type=MESH
        )
        copy.start()
        halo_copies.append(copy)

    grid = jnp.concatenate(
        [jnp.broadcast_to(pick_row, (4, PICKS)), jnp.broadcast_to(pick_col, (4, PICKS))], axis=0
    ).astype(F32)
    grid = grid.T
    rows_k, cols_k = grid[:, 0:1], grid[:, 4:5]
    d = iota((1, 128), 1)
    row0 = (((d >> 5) * 2) * ROWS).astype(F32)
    col0 = ((((d >> 3) & 3) * 8 + (d & 7)) * COLS).astype(F32)
    most = jnp.zeros((1, 128), F32)
    for half in range(2):
        over = touches(rows_k, cols_k, row0 + half * ROWS, col0).astype(F32)
        most = jnp.maximum(most, jnp.sum(over, axis=0, keepdims=True))
    most_ref[0] = jnp.max(most).astype(jnp.int32)
    over = touches(rows_k, cols_k, row0 + (core * ROWS).astype(F32), col0)
    earlier = (iota((PICKS, PICKS), 1) < iota((PICKS, PICKS), 0)).astype(F32).astype(BF16)
    ranks = dot(earlier, over.astype(F32).astype(BF16))
    ranks = jnp.where(over, jnp.minimum(ranks, 64.0), 100.0).astype(BF16)
    spread = ((iota((128, 1024), 1) >> 3) == iota((128, 1024), 0)).astype(F32).astype(BF16)
    onehot[...] = (
        (dot(ranks, spread) == (iota((PICKS, 1024), 1) & 7).astype(F32)).astype(F32).astype(BF16)
    )

    def pool(i, _):
        at = pl.multiple_of(i * WIDE, 8)
        down_sum = raw[pl.ds(at + WIDE, WIDE), :] + raw[pl.ds(at + 2 * WIDE, WIDE), :]
        slot = lax.rem(i, 4)
        band[slot] = down_sum + raw[pl.ds(at + 3 * WIDE, WIDE), :]
        across = band[slot, 7 : 7 + COLS] + band[slot, 8 : 8 + COLS] + band[slot, 9 : 9 + COLS]
        pooled[pl.ds(pl.multiple_of(i * COLS, COLS), COLS), :] = across
        return 0

    lax.fori_loop(0, ROWS, pool, 0, unroll=4)

    pltpu.make_async_copy(line.at[pl.ds(0, 7)], line.at[pl.ds(0, 7)], recv_sem.at[0]).wait()
    me = x * 4 + y

    def send_plane(step, _):
        pltpu.make_async_remote_copy(
            line, plane.at[me], send_sem.at[1], recv_sem.at[1],
            device_id=on_plane(step), device_id_type=MESH,
        ).start()
        return 0

    lax.fori_loop(1, 16, send_plane, 0)
    plane[me] = line[...]

    for copy in halo_copies:
        copy.wait_recv()
    has_up, has_down = (r > 0).astype(F32), (r < 7).astype(F32)
    has_left, has_right = (c > 0).astype(F32), (c < 31).astype(F32)
    side[0] = from_left[...] * has_left
    side[1] = from_right[...] * has_right
    side[0, 0:1] += corner[0, 0:1] * (has_up * has_left)
    side[1, 0:1] += corner[1, 0:1] * (has_up * has_right)
    side[0, 31:32] += corner[2, 0:1] * (has_down * has_left)
    side[1, 31:32] += corner[3, 0:1] * (has_down * has_right)
    pooled[0:COLS] += from_up[...] * has_up
    pooled[(ROWS - 1) * COLS :] += from_down[...] * has_down
    sub = iota((COLS, D_PROJ), 0)

    def lay_out(i, _):
        at = pl.multiple_of(i * COLS, COLS)
        one = pooled[pl.ds(at, COLS), :]
        one += jnp.where(sub == 0, side[0, pl.ds(i, 1), :], 0.0)
        one += jnp.where(sub == COLS - 1, side[1, pl.ds(i, 1), :], 0.0)
        flipped = one.T
        own_sq[pl.ds(i, 1), :] = jnp.sum(flipped * flipped, axis=0, keepdims=True)
        high = flipped.astype(BF16)
        low = (flipped - high.astype(F32)).astype(BF16)
        rhs[0:128, pl.ds(at, COLS)] = high
        rhs[128:256, pl.ds(at, COLS)] = low
        rhs[256:384, pl.ds(at, COLS)] = high
        return 0

    lax.fori_loop(0, ROWS, lay_out, 0, unroll=2)

    pltpu.make_async_copy(plane.at[pl.ds(0, 15)], plane.at[pl.ds(0, 15)], recv_sem.at[1]).wait()
    got = plane[...].reshape(1024, D_PROJ)
    high = got.astype(BF16)
    low = (got - high.astype(F32)).astype(BF16)
    both = dot(onehot[...], jnp.concatenate([high, low], axis=1))
    part[...] = both[:, :D_PROJ] + both[:, D_PROJ:]
    swap = pltpu.make_async_remote_copy(
        part, other, send_sem.at[2], recv_sem.at[2],
        device_id=(x * 2 + 1 - core, c), device_id_type=MESH,
    )
    swap.start()
    swap.wait_recv()

    picks = part[...] + other[...]
    high = picks.astype(BF16)
    lhs[:, 0:128] = high
    lhs[:, 128:256] = high
    lhs[:, 256:384] = (picks - high.astype(F32)).astype(BF16)
    half_sq = jnp.sum(picks * picks, axis=1, keepdims=True) * 0.5
    for i in range(ROWS // 2):
        score = dot(lhs[...], rhs[:, i * 256 : (i + 1) * 256]) - half_sq
        score = jnp.max(score, axis=0, keepdims=True)
        best[2 * i : 2 * i + 1] = score[:, :128]
        best[2 * i + 1 : 2 * i + 2] = score[:, 128:]
    gap = (own_sq[...] - 2.0 * best[...]) * (1.0 / (81.0 * D_PROJ))
    out_ref[...] = jnp.where(valid_ref[...] == 1, jnp.minimum(prev_ref[...], gap), 0.0)

    pltpu.make_async_copy(line.at[pl.ds(0, 7)], line.at[pl.ds(0, 7)], send_sem.at[0]).wait()
    pltpu.make_async_copy(plane.at[pl.ds(0, 15)], plane.at[pl.ds(0, 15)], send_sem.at[1]).wait()
    swap.wait_send()
    for copy in halo_copies:
        copy.wait_send()


def shards(features, projection, prev_dist, valid, pick_owner, pick_slot):
    vmem = pl.BlockSpec(memory_space=pltpu.VMEM)
    result, most = pl.pallas_call(
        kernel,
        out_shape=(
            jax.ShapeDtypeStruct((ROWS, COLS), F32),
            jax.ShapeDtypeStruct((1,), jnp.int32),
        ),
        in_specs=[pl.BlockSpec(memory_space=pltpu.HBM)] + [vmem] * 5,
        out_specs=(vmem, pl.BlockSpec(memory_space=pltpu.SMEM)),
        scratch_shapes=[
            pltpu.VMEM((ROWS, COLS, CHANNELS), BF16),
            pltpu.VMEM((TABLE, D_PROJ), F32),
            pltpu.VMEM((4, WIDE, D_PROJ), F32),
            pltpu.VMEM((ROWS * COLS, D_PROJ), F32),
            pltpu.VMEM((2, COLS, D_PROJ), F32),
            pltpu.VMEM((2, 48, D_PROJ), F32),
            pltpu.VMEM((2, 48, D_PROJ), F32),
            pltpu.VMEM((SLOTS, D_PROJ), F32),
            pltpu.VMEM((8, SLOTS, D_PROJ), F32),
            pltpu.VMEM((16, 8, SLOTS, D_PROJ), F32),
            pltpu.VMEM((PICKS, D_PROJ), F32),
            pltpu.VMEM((PICKS, D_PROJ), F32),
            pltpu.VMEM((PICKS, 1024), BF16),
            pltpu.VMEM((384, ROWS * COLS), BF16),
            pltpu.VMEM((PICKS, 384), BF16),
            pltpu.VMEM((ROWS, COLS), F32),
            pltpu.VMEM((ROWS, COLS), F32),
            pltpu.VMEM((COLS, D_PROJ), F32),
            pltpu.VMEM((COLS, D_PROJ), F32),
            pltpu.VMEM((ROWS, D_PROJ), F32),
            pltpu.VMEM((ROWS, D_PROJ), F32),
            pltpu.VMEM((4, 8, D_PROJ), F32),
            pltpu.VMEM((2, ROWS, D_PROJ), F32),
            pltpu.SemaphoreType.DMA((CHUNKS,)),
            pltpu.SemaphoreType.DMA((3,)),
            pltpu.SemaphoreType.DMA((3,)),
            pltpu.SemaphoreType.DMA((8,)),
            pltpu.SemaphoreType.DMA((8,)),
        ],
        compiler_params=pltpu.CompilerParams(
            collective_id=0, has_side_effects=True, vmem_limit_bytes=56 << 20
        ),
        name="coreset",
    )(
        features, projection, prev_dist, valid,
        pick_owner.reshape(1, PICKS), pick_slot.reshape(1, PICKS),
    )
    return lax.cond(
        most[0] > SLOTS,
        any_picks,
        lambda *_: result,
        features, projection, prev_dist, valid, pick_owner, pick_slot,
    )


def solution(mesh):
    return jax.shard_map(
        shards,
        mesh=mesh,
        in_specs=(P("rows", "cols", None), P(), P("rows", "cols"), P("rows", "cols"), P(), P()),
        out_specs=P("rows", "cols"),
        check_vma=False,
    )
```

```python
import jax
import jax.numpy as jnp
from jax import lax
from jax.experimental import pallas as pl
from jax.experimental.pallas import tpu as pltpu
from jax.sharding import PartitionSpec as P

D_PROJ = 128
MESH = pl.DeviceIdType.MESH
F32, BF16 = jnp.float32, jnp.bfloat16

ROWS, COLS, CHANNELS, PICKS = 32, 128, 1536, 512
SLOTS = 8
CHUNK = 256
CHUNKS = CHANNELS // CHUNK
AHEAD = 3
BAND = 8
WIDE = COLS + 16
TABLE = (ROWS + 4) * WIDE


def padded_2(block, sides, width):
    for axis, dim in sides:
        count = lax.axis_size(axis)
        forward = [(i, i + 1) for i in range(count - 1)]
        backward = [(target, source) for source, target in forward]
        low = lax.ppermute(
            lax.slice_in_dim(block, block.shape[dim] - width, None, axis=dim), axis, forward
        )
        high = lax.ppermute(lax.slice_in_dim(block, 0, width, axis=dim), axis, backward)
        block = jnp.concatenate([low, block, high], axis=dim)
    return block


def window_sum(padded, rows_dev, cols_dev):
    total = jnp.zeros((rows_dev, cols_dev, padded.shape[2]), jnp.float32)
    for row_off in range(3):
        for col_off in range(3):
            total = total + padded[
                row_off : row_off + rows_dev, col_off : col_off + cols_dev
            ].astype(jnp.float32)
    return total / 9.0


def any_picks(features, projection, prev_dist, valid, pick_owner, pick_slot):
    rows_dev, cols_dev, channels = features.shape
    proj_full = projection.astype(jnp.float32)
    own_index = lax.axis_index("rows") * lax.axis_size("cols") + lax.axis_index("cols")
    owned = pick_owner == own_index
    padded = padded_2(features, (("rows", 0), ("cols", 1)), 1)
    pooled = window_sum(padded, rows_dev, cols_dev).reshape(rows_dev * cols_dev, channels)
    projected = jnp.dot(pooled, proj_full, precision=lax.Precision.HIGHEST)
    local_rows = jnp.where(owned[:, None], projected[pick_slot], jnp.float32(0.0))
    pick_rows = local_rows
    for axis in ("rows", "cols"):
        count, step = lax.axis_size(axis), 1
        while step < count:
            swap = [(i, i ^ step) for i in range(count)]
            pick_rows = pick_rows + lax.ppermute(pick_rows, axis, swap)
            step *= 2
    pick_sq = jnp.sum(pick_rows * pick_rows, axis=1)
    own_sq = jnp.sum(projected * projected, axis=1)
    inner_prod = jnp.dot(projected, pick_rows.T, precision=lax.Precision.HIGHEST)
    scaled_gap = (own_sq[:, None] + pick_sq[None, :] - 2.0 * inner_prod) / D_PROJ
    nearest = jnp.min(scaled_gap, axis=1).reshape(rows_dev, cols_dev)
    return jnp.where(valid == 1, jnp.minimum(prev_dist, nearest), jnp.float32(0.0))


def iota(shape, dim):
    return lax.broadcasted_iota(jnp.int32, shape, dim)


def dot(a, b):
    return jnp.dot(a, b, preferred_element_type=F32)


def touches(pick_row, pick_col, row0, col0):
    down, across = pick_row - row0, pick_col - col0
    return (down >= -1) & (down <= ROWS) & (across >= -1) & (across <= COLS)


def kernel(
    feat_hbm, proj_hbm, prev_hbm, valid_hbm, owner_hbm, slot_hbm, out_ref, most_ref,
    owner_ref, slot_ref, proj_ref, prev_ref, valid_ref,
    feat, raw, band, pooled, hrow, ends, mine, line, plane, part, other, onehot,
    rhs, lhs, own_sq, best, from_up, from_down, from_left, from_right, corner, side,
    load_sem, small_sem, send_sem, recv_sem, halo_send, halo_recv,
):
    r, c = lax.axis_index("rows"), lax.axis_index("cols")
    x, core = r // 2, r % 2
    y, z = c // 8, c % 8
    up, down = lax.rem(r + 7, 8), lax.rem(r + 1, 8)
    left, right = lax.rem(c + 31, 32), lax.rem(c + 1, 32)

    def on_line(step):
        return (r, y * 8 + lax.rem(z + step, 8))

    def on_plane(step):
        return (lax.rem(x + step // 4, 4) * 2 + core, lax.rem(y + step % 4, 4) * 8 + z)

    loads = [
        pltpu.make_async_copy(feat_hbm.at[:, :, pl.ds(i * CHUNK, CHUNK)], feat.at[i], load_sem.at[i])
        for i in range(CHUNKS)
    ]
    smalls = [
        pltpu.make_async_copy(source, target, small_sem.at[n])
        for n, (source, target) in enumerate(
            (
                (owner_hbm, owner_ref),
                (slot_hbm, slot_ref),
                (proj_hbm, proj_ref),
                (prev_hbm, prev_ref),
                (valid_hbm, valid_ref),
            )
        )
    ]
    for load in smalls[:3] + loads[:AHEAD] + smalls[3:]:
        load.start()

    barrier = pltpu.get_barrier_semaphore()

    def greet(device):
        pl.semaphore_signal(barrier, inc=1, device_id=device, device_id_type=MESH)

    def greet_line(step, _):
        greet(on_line(step))
        return 0

    def greet_plane(step, _):
        greet(on_plane(step))
        return 0

    lax.fori_loop(1, 8, greet_line, 0)
    lax.fori_loop(1, 16, greet_plane, 0)
    around = [(up, c), (down, c), (r, left), (r, right)]
    around += [(up, left), (up, right), (down, left), (down, right)]
    for device in around:
        greet(device)

    smalls[0].wait()
    smalls[1].wait()
    owner, slot = owner_ref[...], slot_ref[...]
    pick_row = (owner >> 5) * ROWS + (slot >> 7)
    pick_col = (owner & 31) * COLS + (slot & 127)
    here = jnp.broadcast_to(touches(pick_row, pick_col, r * ROWS, c * COLS), (8, PICKS))
    before = (iota((PICKS, PICKS), 0) < iota((PICKS, PICKS), 1)).astype(F32).astype(BF16)
    rank = dot(here.astype(F32).astype(BF16), before)
    tile_row, tile_col = pick_row - r * ROWS, pick_col - c * COLS
    place = (tile_row + 2) * WIDE + tile_col + 8
    chosen = here & (rank == iota((8, PICKS), 0).astype(F32))
    places = jnp.sum(
        jnp.where(chosen, jnp.broadcast_to(place, (8, PICKS)).astype(F32), 0.0), axis=1, keepdims=True
    ).astype(jnp.int32)
    places = jnp.clip(places, WIDE + 1, TABLE - WIDE - 2)
    filled = jnp.sum(chosen.astype(F32), axis=1, keepdims=True)

    raw[0 : 2 * WIDE] = jnp.zeros((2 * WIDE, D_PROJ), F32)
    raw[TABLE - 2 * WIDE :] = jnp.zeros((2 * WIDE, D_PROJ), F32)
    smalls[2].wait()
    proj = proj_ref[...]
    margin = jnp.zeros((8, D_PROJ), F32)
    for row in range(2, ROWS + 2):
        raw[row * WIDE : row * WIDE + 8] = margin
        raw[row * WIDE + 8 + COLS : (row + 1) * WIDE] = margin
    for i in range(CHUNKS):
        loads[i].wait()
        if i + AHEAD < CHUNKS:
            loads[i + AHEAD].start()
        for top in range(0, ROWS, BAND):
            block = feat[i, top : top + BAND].reshape(BAND * COLS, CHUNK)
            done = dot(block, proj[i * CHUNK : (i + 1) * CHUNK])
            for k in range(BAND):
                at = (top + k + 2) * WIDE + 8
                one = done[k * COLS : (k + 1) * COLS]
                raw[at : at + COLS] = one if i == 0 else raw[at : at + COLS] + one

    for j in range(SLOTS):
        place = places[j, 0]
        near = raw[pl.ds(place - WIDE - 1, 3), :] + raw[pl.ds(place - 1, 3), :]
        near += raw[pl.ds(place + WIDE - 1, 3), :]
        mine[j : j + 1] = near[0:1] + near[1:2] + near[2:3]
    mine[...] = jnp.where(filled > 0.0, mine[...], 0.0)
    line[z] = mine[...]

    pl.semaphore_wait(barrier, 30)

    def send_line(step, _):
        pltpu.make_async_remote_copy(
            mine, line.at[z], send_sem.at[0], recv_sem.at[0],
            device_id=on_line(step), device_id_type=MESH,
        ).start()
        return 0

    lax.fori_loop(1, 8, send_line, 0)

    for n, at in enumerate((2 * WIDE, (ROWS + 1) * WIDE)):
        hrow[n] = raw[at + 7 : at + 7 + COLS] + raw[at + 8 : at + 8 + COLS] + raw[at + 9 : at + 9 + COLS]
    for n in range(2):
        first = 2 * WIDE + 8 + n * (COLS - 1)
        inner = raw[pl.ds(first, ROWS, stride=WIDE), :]
        outer = raw[pl.ds(first - WIDE, ROWS, stride=WIDE), :]
        outer += raw[pl.ds(first + WIDE, ROWS, stride=WIDE), :]
        ends[n, 0:32] = inner + outer
        ends[n, 32:40] = jnp.broadcast_to(inner[0:1], (8, D_PROJ))
        ends[n, 40:48] = jnp.broadcast_to(inner[ROWS - 1 :], (8, D_PROJ))
    halos = [
        (hrow.at[0], from_down, (up, c)),
        (hrow.at[1], from_up, (down, c)),
        (ends.at[0, pl.ds(0, 32)], from_right, (r, left)),
        (ends.at[1, pl.ds(0, 32)], from_left, (r, right)),
        (ends.at[0, pl.ds(32, 8)], corner.at[3], (up, left)),
        (ends.at[1, pl.ds(32, 8)], corner.at[2], (up, right)),
        (ends.at[0, pl.ds(40, 8)], corner.at[1], (down, left)),
        (ends.at[1, pl.ds(40, 8)], corner.at[0], (down, right)),
    ]
    halo_copies = []
    for n, (source, target, device) in enumerate(halos):
        copy = pltpu.make_async_remote_copy(
            source, target, halo_send.at[n], halo_recv.at[n], device_id=device, device_id_type=MESH
        )
        copy.start()
        halo_copies.append(copy)

    grid = jnp.concatenate(
        [jnp.broadcast_to(pick_row, (4, PICKS)), jnp.broadcast_to(pick_col, (4, PICKS))], axis=0
    ).astype(F32)
    grid = grid.T
    rows_k, cols_k = grid[:, 0:1], grid[:, 4:5]
    d = iota((1, 128), 1)
    row0 = (((d >> 5) * 2) * ROWS).astype(F32)
    col0 = ((((d >> 3) & 3) * 8 + (d & 7)) * COLS).astype(F32)
    most = jnp.zeros((1, 128), F32)
    for half in range(2):
        over = touches(rows_k, cols_k, row0 + half * ROWS, col0).astype(F32)
        most = jnp.maximum(most, jnp.sum(over, axis=0, keepdims=True))
    most_ref[0] = jnp.max(most).astype(jnp.int32)
    over = touches(rows_k, cols_k, row0 + (core * ROWS).astype(F32), col0)
    earlier = (iota((PICKS, PICKS), 1) < iota((PICKS, PICKS), 0)).astype(F32).astype(BF16)
    ranks = dot(earlier, over.astype(F32).astype(BF16))
    ranks = jnp.where(over, jnp.minimum(ranks, 64.0), 100.0).astype(BF16)
    spread = ((iota((128, 1024), 1) >> 3) == iota((128, 1024), 0)).astype(F32).astype(BF16)
    onehot[...] = (
        (dot(ranks, spread) == (iota((PICKS, 1024), 1) & 7).astype(F32)).astype(F32).astype(BF16)
    )

    def pool(i, _):
        at = pl.multiple_of(i * WIDE, 8)
        down_sum = raw[pl.ds(at + WIDE, WIDE), :] + raw[pl.ds(at + 2 * WIDE, WIDE), :]
        slot = lax.rem(i, 4)
        band[slot] = down_sum + raw[pl.ds(at + 3 * WIDE, WIDE), :]
        across = band[slot, 7 : 7 + COLS] + band[slot, 8 : 8 + COLS] + band[slot, 9 : 9 + COLS]
        pooled[pl.ds(pl.multiple_of(i * COLS, COLS), COLS), :] = across
        return 0

    lax.fori_loop(0, ROWS, pool, 0, unroll=4)

    pltpu.make_async_copy(line.at[pl.ds(0, 7)], line.at[pl.ds(0, 7)], recv_sem.at[0]).wait()
    me = x * 4 + y

    def send_plane(step, _):
        pltpu.make_async_remote_copy(
            line, plane.at[me], send_sem.at[1], recv_sem.at[1],
            device_id=on_plane(step), device_id_type=MESH,
        ).start()
        return 0

    lax.fori_loop(1, 16, send_plane, 0)
    plane[me] = line[...]

    for copy in halo_copies:
        copy.wait_recv()
    has_up, has_down = (r > 0).astype(F32), (r < 7).astype(F32)
    has_left, has_right = (c > 0).astype(F32), (c < 31).astype(F32)
    side[0] = from_left[...] * has_left
    side[1] = from_right[...] * has_right
    side[0, 0:1] += corner[0, 0:1] * (has_up * has_left)
    side[1, 0:1] += corner[1, 0:1] * (has_up * has_right)
    side[0, 31:32] += corner[2, 0:1] * (has_down * has_left)
    side[1, 31:32] += corner[3, 0:1] * (has_down * has_right)
    pooled[0:COLS] += from_up[...] * has_up
    pooled[(ROWS - 1) * COLS :] += from_down[...] * has_down
    sub = iota((COLS, D_PROJ), 0)

    def lay_out(i, _):
        at = pl.multiple_of(i * COLS, COLS)
        one = pooled[pl.ds(at, COLS), :]
        one += jnp.where(sub == 0, side[0, pl.ds(i, 1), :], 0.0)
        one += jnp.where(sub == COLS - 1, side[1, pl.ds(i, 1), :], 0.0)
        flipped = one.T
        own_sq[pl.ds(i, 1), :] = jnp.sum(flipped * flipped, axis=0, keepdims=True)
        high = flipped.astype(BF16)
        low = (flipped - high.astype(F32)).astype(BF16)
        rhs[0:128, pl.ds(at, COLS)] = high
        rhs[128:256, pl.ds(at, COLS)] = low
        rhs[256:384, pl.ds(at, COLS)] = high
        return 0

    lax.fori_loop(0, ROWS, lay_out, 0, unroll=2)

    pltpu.make_async_copy(plane.at[pl.ds(0, 15)], plane.at[pl.ds(0, 15)], recv_sem.at[1]).wait()
    got = plane[...].reshape(1024, D_PROJ)
    high = got.astype(BF16)
    low = (got - high.astype(F32)).astype(BF16)
    both = dot(onehot[...], jnp.concatenate([high, low], axis=1))
    part[...] = both[:, :D_PROJ] + both[:, D_PROJ:]
    swap = pltpu.make_async_remote_copy(
        part, other, send_sem.at[2], recv_sem.at[2],
        device_id=(x * 2 + 1 - core, c), device_id_type=MESH,
    )
    swap.start()
    swap.wait_recv()

    picks = part[...] + other[...]
    high = picks.astype(BF16)
    lhs[:, 0:128] = high
    lhs[:, 128:256] = high
    lhs[:, 256:384] = (picks - high.astype(F32)).astype(BF16)
    half_sq = jnp.sum(picks * picks, axis=1, keepdims=True) * 0.5
    for i in range(ROWS // 2):
        score = dot(lhs[...], rhs[:, i * 256 : (i + 1) * 256]) - half_sq
        score = jnp.max(score, axis=0, keepdims=True)
        best[2 * i : 2 * i + 1] = score[:, :128]
        best[2 * i + 1 : 2 * i + 2] = score[:, 128:]
    smalls[3].wait()
    smalls[4].wait()
    gap = (own_sq[...] - 2.0 * best[...]) * (1.0 / (81.0 * D_PROJ))
    out_ref[...] = jnp.where(valid_ref[...] == 1, jnp.minimum(prev_ref[...], gap), 0.0)

    pltpu.make_async_copy(line.at[pl.ds(0, 7)], line.at[pl.ds(0, 7)], send_sem.at[0]).wait()
    pltpu.make_async_copy(plane.at[pl.ds(0, 15)], plane.at[pl.ds(0, 15)], send_sem.at[1]).wait()
    swap.wait_send()
    for copy in halo_copies:
        copy.wait_send()


def shards(features, projection, prev_dist, valid, pick_owner, pick_slot):
    vmem = pl.BlockSpec(memory_space=pltpu.VMEM)
    result, most = pl.pallas_call(
        kernel,
        out_shape=(
            jax.ShapeDtypeStruct((ROWS, COLS), F32),
            jax.ShapeDtypeStruct((1,), jnp.int32),
        ),
        in_specs=[pl.BlockSpec(memory_space=pltpu.HBM)] * 6,
        out_specs=(vmem, pl.BlockSpec(memory_space=pltpu.SMEM)),
        scratch_shapes=[
            pltpu.VMEM((1, PICKS), jnp.int32),
            pltpu.VMEM((1, PICKS), jnp.int32),
            pltpu.VMEM((CHANNELS, D_PROJ), BF16),
            pltpu.VMEM((ROWS, COLS), F32),
            pltpu.VMEM((ROWS, COLS), jnp.int32),
            pltpu.VMEM((CHUNKS, ROWS, COLS, CHUNK), BF16),
            pltpu.VMEM((TABLE, D_PROJ), F32),
            pltpu.VMEM((4, WIDE, D_PROJ), F32),
            pltpu.VMEM((ROWS * COLS, D_PROJ), F32),
            pltpu.VMEM((2, COLS, D_PROJ), F32),
            pltpu.VMEM((2, 48, D_PROJ), F32),
            pltpu.VMEM((SLOTS, D_PROJ), F32),
            pltpu.VMEM((8, SLOTS, D_PROJ), F32),
            pltpu.VMEM((16, 8, SLOTS, D_PROJ), F32),
            pltpu.VMEM((PICKS, D_PROJ), F32),
            pltpu.VMEM((PICKS, D_PROJ), F32),
            pltpu.VMEM((PICKS, 1024), BF16),
            pltpu.VMEM((384, ROWS * COLS), BF16),
            pltpu.VMEM((PICKS, 384), BF16),
            pltpu.VMEM((ROWS, COLS), F32),
            pltpu.VMEM((ROWS, COLS), F32),
            pltpu.VMEM((COLS, D_PROJ), F32),
            pltpu.VMEM((COLS, D_PROJ), F32),
            pltpu.VMEM((ROWS, D_PROJ), F32),
            pltpu.VMEM((ROWS, D_PROJ), F32),
            pltpu.VMEM((4, 8, D_PROJ), F32),
            pltpu.VMEM((2, ROWS, D_PROJ), F32),
            pltpu.SemaphoreType.DMA((CHUNKS,)),
            pltpu.SemaphoreType.DMA((5,)),
            pltpu.SemaphoreType.DMA((3,)),
            pltpu.SemaphoreType.DMA((3,)),
            pltpu.SemaphoreType.DMA((8,)),
            pltpu.SemaphoreType.DMA((8,)),
        ],
        compiler_params=pltpu.CompilerParams(
            collective_id=0, has_side_effects=True, vmem_limit_bytes=56 << 20
        ),
        name="coreset",
    )(
        features, projection, prev_dist, valid,
        pick_owner.reshape(1, PICKS), pick_slot.reshape(1, PICKS),
    )
    return lax.cond(
        most[0] > SLOTS,
        any_picks,
        lambda *_: result,
        features, projection, prev_dist, valid, pick_owner, pick_slot,
    )


def solution(mesh):
    return jax.shard_map(
        shards,
        mesh=mesh,
        in_specs=(P("rows", "cols", None), P(), P("rows", "cols"), P("rows", "cols"), P(), P()),
        out_specs=P("rows", "cols"),
        check_vma=False,
    )
```

```python
import jax
import jax.numpy as jnp
from jax import lax
from jax.experimental import pallas as pl
from jax.experimental.pallas import tpu as pltpu
from jax.sharding import PartitionSpec as P

D_PROJ = 128
MESH = pl.DeviceIdType.MESH
F32, BF16 = jnp.float32, jnp.bfloat16

ROWS, COLS, CHANNELS, PICKS = 32, 128, 1536, 512
SLOTS = 8
LINE_SLOTS = 64
CHUNK = 256
CHUNKS = CHANNELS // CHUNK
AHEAD = 3
BAND = 8
WIDE = COLS + 16
TABLE = (ROWS + 4) * WIDE


def padded_2(block, sides, width):
    for axis, dim in sides:
        count = lax.axis_size(axis)
        forward = [(i, i + 1) for i in range(count - 1)]
        backward = [(target, source) for source, target in forward]
        low = lax.ppermute(
            lax.slice_in_dim(block, block.shape[dim] - width, None, axis=dim), axis, forward
        )
        high = lax.ppermute(lax.slice_in_dim(block, 0, width, axis=dim), axis, backward)
        block = jnp.concatenate([low, block, high], axis=dim)
    return block


def window_sum(padded, rows_dev, cols_dev):
    total = jnp.zeros((rows_dev, cols_dev, padded.shape[2]), jnp.float32)
    for row_off in range(3):
        for col_off in range(3):
            total = total + padded[
                row_off : row_off + rows_dev, col_off : col_off + cols_dev
            ].astype(jnp.float32)
    return total / 9.0


def any_picks(features, projection, prev_dist, valid, pick_owner, pick_slot):
    rows_dev, cols_dev, channels = features.shape
    proj_full = projection.astype(jnp.float32)
    own_index = lax.axis_index("rows") * lax.axis_size("cols") + lax.axis_index("cols")
    owned = pick_owner == own_index
    padded = padded_2(features, (("rows", 0), ("cols", 1)), 1)
    pooled = window_sum(padded, rows_dev, cols_dev).reshape(rows_dev * cols_dev, channels)
    projected = jnp.dot(pooled, proj_full, precision=lax.Precision.HIGHEST)
    local_rows = jnp.where(owned[:, None], projected[pick_slot], jnp.float32(0.0))
    pick_rows = local_rows
    for axis in ("rows", "cols"):
        count, step = lax.axis_size(axis), 1
        while step < count:
            swap = [(i, i ^ step) for i in range(count)]
            pick_rows = pick_rows + lax.ppermute(pick_rows, axis, swap)
            step *= 2
    pick_sq = jnp.sum(pick_rows * pick_rows, axis=1)
    own_sq = jnp.sum(projected * projected, axis=1)
    inner_prod = jnp.dot(projected, pick_rows.T, precision=lax.Precision.HIGHEST)
    scaled_gap = (own_sq[:, None] + pick_sq[None, :] - 2.0 * inner_prod) / D_PROJ
    nearest = jnp.min(scaled_gap, axis=1).reshape(rows_dev, cols_dev)
    return jnp.where(valid == 1, jnp.minimum(prev_dist, nearest), jnp.float32(0.0))


def iota(shape, dim):
    return lax.broadcasted_iota(jnp.int32, shape, dim)


def dot(a, b):
    return jnp.dot(a, b, preferred_element_type=F32)


def touches(pick_row, pick_col, row0, col0, rows=ROWS, cols=COLS):
    down, across = pick_row - row0, pick_col - col0
    return (down >= -1) & (down <= rows) & (across >= -1) & (across <= cols)


def kernel(
    feat_hbm, proj_hbm, prev_hbm, valid_hbm, owner_hbm, slot_hbm, out_ref, most_ref,
    owner_ref, slot_ref, proj_ref, prev_ref, valid_ref,
    feat, raw, band, pooled, hrow, ends, mine, line, packed, plane, onehot,
    rhs, lhs, own_sq, best, from_up, from_down, from_left, from_right, corner, side,
    load_sem, small_sem, send_sem, recv_sem, halo_send, halo_recv,
):
    r, c = lax.axis_index("rows"), lax.axis_index("cols")
    x, core = r // 2, r % 2
    y, z = c // 8, c % 8
    up, down = lax.rem(r + 7, 8), lax.rem(r + 1, 8)
    left, right = lax.rem(c + 31, 32), lax.rem(c + 1, 32)

    def on_line(step):
        return (x * 2 + lax.rem(core + step // 8, 2), y * 8 + lax.rem(z + step % 8, 8))

    def on_plane(step):
        return (lax.rem(x + step // 4, 4) * 2 + core, lax.rem(y + step % 4, 4) * 8 + z)

    loads = [
        pltpu.make_async_copy(feat_hbm.at[:, :, pl.ds(i * CHUNK, CHUNK)], feat.at[i], load_sem.at[i])
        for i in range(CHUNKS)
    ]
    smalls = [
        pltpu.make_async_copy(source, target, small_sem.at[n])
        for n, (source, target) in enumerate(
            (
                (owner_hbm, owner_ref),
                (slot_hbm, slot_ref),
                (proj_hbm, proj_ref),
                (prev_hbm, prev_ref),
                (valid_hbm, valid_ref),
            )
        )
    ]
    for load in smalls[:3] + loads[:AHEAD] + smalls[3:]:
        load.start()

    barrier = pltpu.get_barrier_semaphore()

    def greet(device):
        pl.semaphore_signal(barrier, inc=1, device_id=device, device_id_type=MESH)

    def greet_line(step, _):
        greet(on_line(step))
        return 0

    def greet_plane(step, _):
        greet(on_plane(step))
        return 0

    lax.fori_loop(1, 16, greet_line, 0)
    lax.fori_loop(1, 16, greet_plane, 0)
    around = [(up, c), (down, c), (r, left), (r, right)]
    around += [(up, left), (up, right), (down, left), (down, right)]
    for device in around:
        greet(device)

    smalls[0].wait()
    smalls[1].wait()
    owner, slot = owner_ref[...], slot_ref[...]
    pick_row = (owner >> 5) * ROWS + (slot >> 7)
    pick_col = (owner & 31) * COLS + (slot & 127)
    here = jnp.broadcast_to(touches(pick_row, pick_col, r * ROWS, c * COLS), (8, PICKS))
    before = (iota((PICKS, PICKS), 0) < iota((PICKS, PICKS), 1)).astype(F32).astype(BF16)
    rank = dot(here.astype(F32).astype(BF16), before)
    tile_row, tile_col = pick_row - r * ROWS, pick_col - c * COLS
    place = (tile_row + 2) * WIDE + tile_col + 8
    chosen = here & (rank == iota((8, PICKS), 0).astype(F32))
    places = jnp.sum(
        jnp.where(chosen, jnp.broadcast_to(place, (8, PICKS)).astype(F32), 0.0), axis=1, keepdims=True
    ).astype(jnp.int32)
    places = jnp.clip(places, WIDE + 1, TABLE - WIDE - 2)
    filled = jnp.sum(chosen.astype(F32), axis=1, keepdims=True)

    raw[0 : 2 * WIDE] = jnp.zeros((2 * WIDE, D_PROJ), F32)
    raw[TABLE - 2 * WIDE :] = jnp.zeros((2 * WIDE, D_PROJ), F32)
    smalls[2].wait()
    proj = proj_ref[...]
    margin = jnp.zeros((8, D_PROJ), F32)
    for row in range(2, ROWS + 2):
        raw[row * WIDE : row * WIDE + 8] = margin
        raw[row * WIDE + 8 + COLS : (row + 1) * WIDE] = margin
    for i in range(CHUNKS):
        loads[i].wait()
        if i + AHEAD < CHUNKS:
            loads[i + AHEAD].start()
        for top in range(0, ROWS, BAND):
            block = feat[i, top : top + BAND].reshape(BAND * COLS, CHUNK)
            done = dot(block, proj[i * CHUNK : (i + 1) * CHUNK])
            for k in range(BAND):
                at = (top + k + 2) * WIDE + 8
                one = done[k * COLS : (k + 1) * COLS]
                raw[at : at + COLS] = one if i == 0 else raw[at : at + COLS] + one

    for j in range(SLOTS):
        place = places[j, 0]
        near = raw[pl.ds(place - WIDE - 1, 3), :] + raw[pl.ds(place - 1, 3), :]
        near += raw[pl.ds(place + WIDE - 1, 3), :]
        mine[j : j + 1] = near[0:1] + near[1:2] + near[2:3]
    mine[...] = jnp.where(filled > 0.0, mine[...], 0.0)
    spot = core * 8 + z
    line[spot] = mine[...]

    pl.semaphore_wait(barrier, 38)

    def send_line(step, _):
        pltpu.make_async_remote_copy(
            mine, line.at[spot], send_sem.at[0], recv_sem.at[0],
            device_id=on_line(step), device_id_type=MESH,
        ).start()
        return 0

    lax.fori_loop(1, 16, send_line, 0)

    for n, at in enumerate((2 * WIDE, (ROWS + 1) * WIDE)):
        hrow[n] = raw[at + 7 : at + 7 + COLS] + raw[at + 8 : at + 8 + COLS] + raw[at + 9 : at + 9 + COLS]
    for n in range(2):
        first = 2 * WIDE + 8 + n * (COLS - 1)
        inner = raw[pl.ds(first, ROWS, stride=WIDE), :]
        outer = raw[pl.ds(first - WIDE, ROWS, stride=WIDE), :]
        outer += raw[pl.ds(first + WIDE, ROWS, stride=WIDE), :]
        ends[n, 0:32] = inner + outer
        ends[n, 32:40] = jnp.broadcast_to(inner[0:1], (8, D_PROJ))
        ends[n, 40:48] = jnp.broadcast_to(inner[ROWS - 1 :], (8, D_PROJ))
    halos = [
        (hrow.at[0], from_down, (up, c)),
        (hrow.at[1], from_up, (down, c)),
        (ends.at[0, pl.ds(0, 32)], from_right, (r, left)),
        (ends.at[1, pl.ds(0, 32)], from_left, (r, right)),
        (ends.at[0, pl.ds(32, 8)], corner.at[3], (up, left)),
        (ends.at[1, pl.ds(32, 8)], corner.at[2], (up, right)),
        (ends.at[0, pl.ds(40, 8)], corner.at[1], (down, left)),
        (ends.at[1, pl.ds(40, 8)], corner.at[0], (down, right)),
    ]
    halo_copies = []
    for n, (source, target, device) in enumerate(halos):
        copy = pltpu.make_async_remote_copy(
            source, target, halo_send.at[n], halo_recv.at[n], device_id=device, device_id_type=MESH
        )
        copy.start()
        halo_copies.append(copy)

    grid = jnp.concatenate(
        [jnp.broadcast_to(pick_row, (4, PICKS)), jnp.broadcast_to(pick_col, (4, PICKS))], axis=0
    ).astype(F32)
    grid = grid.T
    rows_k, cols_k = grid[:, 0:1], grid[:, 4:5]
    me = x * 4 + y
    d = iota((1, 128), 1)
    row0 = (((d >> 5) * 2) * ROWS).astype(F32)
    col0 = ((((d >> 3) & 3) * 8 + (d & 7)) * COLS).astype(F32)
    most = jnp.zeros((1, 128), F32)
    for half in range(2):
        over = touches(rows_k, cols_k, row0 + half * ROWS, col0).astype(F32)
        most = jnp.maximum(most, jnp.sum(over, axis=0, keepdims=True))
    earlier = (iota((PICKS, PICKS), 1) < iota((PICKS, PICKS), 0)).astype(F32).astype(BF16)
    row0, col0 = ((d >> 2) * (2 * ROWS)).astype(F32), ((d & 3) * (8 * COLS)).astype(F32)
    over = touches(rows_k, cols_k, row0, col0, 2 * ROWS, 8 * COLS) & (d < 16)
    in_line = jnp.sum(over.astype(F32), axis=0, keepdims=True)
    most_ref[0] = (
        (jnp.max(most) > float(SLOTS)) | (jnp.max(in_line) > float(LINE_SLOTS))
    ).astype(jnp.int32)
    ranks = dot(earlier, over.astype(F32).astype(BF16))
    ranks = jnp.where(over, jnp.minimum(ranks, 100.0), 200.0)
    spread = ((iota((128, 1024), 1) >> 6) == iota((128, 1024), 0)).astype(F32).astype(BF16)
    onehot[...] = (
        (dot(ranks.astype(BF16), spread) == (iota((PICKS, 1024), 1) & 63).astype(F32))
        .astype(F32)
        .astype(BF16)
    )
    here = jnp.sum(jnp.where(d == me, ranks, 0.0), axis=1, keepdims=True)
    goes = (here == iota((PICKS, 128), 1).astype(F32)).astype(F32).T[:LINE_SLOTS].astype(BF16)
    row0 = ((x * 2 + (d >> 6)) * ROWS).astype(F32)
    col0 = ((y * 8 + ((d >> 3) & 7)) * COLS).astype(F32)
    over = touches(rows_k, cols_k, row0, col0)
    ranks = dot(earlier, over.astype(F32).astype(BF16))
    comes = (over & (ranks == (d & 7).astype(F32))).astype(F32).astype(BF16)
    gather = dot(goes, comes).astype(BF16)

    def pool(i, _):
        at = pl.multiple_of(i * WIDE, 8)
        down_sum = raw[pl.ds(at + WIDE, WIDE), :] + raw[pl.ds(at + 2 * WIDE, WIDE), :]
        slot = lax.rem(i, 4)
        band[slot] = down_sum + raw[pl.ds(at + 3 * WIDE, WIDE), :]
        across = band[slot, 7 : 7 + COLS] + band[slot, 8 : 8 + COLS] + band[slot, 9 : 9 + COLS]
        pooled[pl.ds(pl.multiple_of(i * COLS, COLS), COLS), :] = across
        return 0

    lax.fori_loop(0, ROWS, pool, 0, unroll=4)

    pltpu.make_async_copy(line.at[pl.ds(0, 15)], line.at[pl.ds(0, 15)], recv_sem.at[0]).wait()
    got = line[...].reshape(128, D_PROJ)
    high = got.astype(BF16)
    rest = got - high.astype(F32)
    middle = rest.astype(BF16)
    low = (rest - middle.astype(F32)).astype(BF16)
    three = dot(gather, jnp.concatenate([high, middle, low], axis=1))
    packed[...] = three[:, :D_PROJ] + three[:, D_PROJ : 2 * D_PROJ] + three[:, 2 * D_PROJ :]

    def send_plane(step, _):
        pltpu.make_async_remote_copy(
            packed, plane.at[me], send_sem.at[1], recv_sem.at[1],
            device_id=on_plane(step), device_id_type=MESH,
        ).start()
        return 0

    lax.fori_loop(1, 16, send_plane, 0)
    plane[me] = packed[...]

    for copy in halo_copies:
        copy.wait_recv()
    has_up, has_down = (r > 0).astype(F32), (r < 7).astype(F32)
    has_left, has_right = (c > 0).astype(F32), (c < 31).astype(F32)
    side[0] = from_left[...] * has_left
    side[1] = from_right[...] * has_right
    side[0, 0:1] += corner[0, 0:1] * (has_up * has_left)
    side[1, 0:1] += corner[1, 0:1] * (has_up * has_right)
    side[0, 31:32] += corner[2, 0:1] * (has_down * has_left)
    side[1, 31:32] += corner[3, 0:1] * (has_down * has_right)
    pooled[0:COLS] += from_up[...] * has_up
    pooled[(ROWS - 1) * COLS :] += from_down[...] * has_down
    sub = iota((COLS, D_PROJ), 0)

    def lay_out(i, _):
        at = pl.multiple_of(i * COLS, COLS)
        one = pooled[pl.ds(at, COLS), :]
        one += jnp.where(sub == 0, side[0, pl.ds(i, 1), :], 0.0)
        one += jnp.where(sub == COLS - 1, side[1, pl.ds(i, 1), :], 0.0)
        flipped = one.T
        own_sq[pl.ds(i, 1), :] = jnp.sum(flipped * flipped, axis=0, keepdims=True)
        high = flipped.astype(BF16)
        low = (flipped - high.astype(F32)).astype(BF16)
        rhs[0:128, pl.ds(at, COLS)] = high
        rhs[128:256, pl.ds(at, COLS)] = low
        rhs[256:384, pl.ds(at, COLS)] = high
        return 0

    lax.fori_loop(0, ROWS, lay_out, 0, unroll=2)

    pltpu.make_async_copy(plane.at[pl.ds(0, 15)], plane.at[pl.ds(0, 15)], recv_sem.at[1]).wait()
    got = plane[...].reshape(1024, D_PROJ)
    high = got.astype(BF16)
    low = (got - high.astype(F32)).astype(BF16)
    both = dot(onehot[...], jnp.concatenate([high, low], axis=1))
    picks = both[:, :D_PROJ] + both[:, D_PROJ:]
    high = picks.astype(BF16)
    lhs[:, 0:128] = high
    lhs[:, 128:256] = high
    lhs[:, 256:384] = (picks - high.astype(F32)).astype(BF16)
    half_sq = jnp.sum(picks * picks, axis=1, keepdims=True) * 0.5
    for i in range(ROWS // 2):
        score = dot(lhs[...], rhs[:, i * 256 : (i + 1) * 256]) - half_sq
        score = jnp.max(score, axis=0, keepdims=True)
        best[2 * i : 2 * i + 1] = score[:, :128]
        best[2 * i + 1 : 2 * i + 2] = score[:, 128:]
    smalls[3].wait()
    smalls[4].wait()
    gap = (own_sq[...] - 2.0 * best[...]) * (1.0 / (81.0 * D_PROJ))
    out_ref[...] = jnp.where(valid_ref[...] == 1, jnp.minimum(prev_ref[...], gap), 0.0)

    pltpu.make_async_copy(line.at[pl.ds(0, 15)], line.at[pl.ds(0, 15)], send_sem.at[0]).wait()
    pltpu.make_async_copy(plane.at[pl.ds(0, 15)], plane.at[pl.ds(0, 15)], send_sem.at[1]).wait()
    for copy in halo_copies:
        copy.wait_send()


def shards(features, projection, prev_dist, valid, pick_owner, pick_slot):
    vmem = pl.BlockSpec(memory_space=pltpu.VMEM)
    result, most = pl.pallas_call(
        kernel,
        out_shape=(
            jax.ShapeDtypeStruct((ROWS, COLS), F32),
            jax.ShapeDtypeStruct((1,), jnp.int32),
        ),
        in_specs=[pl.BlockSpec(memory_space=pltpu.HBM)] * 6,
        out_specs=(vmem, pl.BlockSpec(memory_space=pltpu.SMEM)),
        scratch_shapes=[
            pltpu.VMEM((1, PICKS), jnp.int32),
            pltpu.VMEM((1, PICKS), jnp.int32),
            pltpu.VMEM((CHANNELS, D_PROJ), BF16),
            pltpu.VMEM((ROWS, COLS), F32),
            pltpu.VMEM((ROWS, COLS), jnp.int32),
            pltpu.VMEM((CHUNKS, ROWS, COLS, CHUNK), BF16),
            pltpu.VMEM((TABLE, D_PROJ), F32),
            pltpu.VMEM((4, WIDE, D_PROJ), F32),
            pltpu.VMEM((ROWS * COLS, D_PROJ), F32),
            pltpu.VMEM((2, COLS, D_PROJ), F32),
            pltpu.VMEM((2, 48, D_PROJ), F32),
            pltpu.VMEM((SLOTS, D_PROJ), F32),
            pltpu.VMEM((16, SLOTS, D_PROJ), F32),
            pltpu.VMEM((LINE_SLOTS, D_PROJ), F32),
            pltpu.VMEM((16, LINE_SLOTS, D_PROJ), F32),
            pltpu.VMEM((PICKS, 1024), BF16),
            pltpu.VMEM((384, ROWS * COLS), BF16),
            pltpu.VMEM((PICKS, 384), BF16),
            pltpu.VMEM((ROWS, COLS), F32),
            pltpu.VMEM((ROWS, COLS), F32),
            pltpu.VMEM((COLS, D_PROJ), F32),
            pltpu.VMEM((COLS, D_PROJ), F32),
            pltpu.VMEM((ROWS, D_PROJ), F32),
            pltpu.VMEM((ROWS, D_PROJ), F32),
            pltpu.VMEM((4, 8, D_PROJ), F32),
            pltpu.VMEM((2, ROWS, D_PROJ), F32),
            pltpu.SemaphoreType.DMA((CHUNKS,)),
            pltpu.SemaphoreType.DMA((5,)),
            pltpu.SemaphoreType.DMA((2,)),
            pltpu.SemaphoreType.DMA((2,)),
            pltpu.SemaphoreType.DMA((8,)),
            pltpu.SemaphoreType.DMA((8,)),
        ],
        compiler_params=pltpu.CompilerParams(
            collective_id=0, has_side_effects=True, vmem_limit_bytes=56 << 20
        ),
        name="coreset",
    )(
        features, projection, prev_dist, valid,
        pick_owner.reshape(1, PICKS), pick_slot.reshape(1, PICKS),
    )
    return lax.cond(
        most[0] > 0,
        any_picks,
        lambda *_: result,
        features, projection, prev_dist, valid, pick_owner, pick_slot,
    )


def solution(mesh):
    return jax.shard_map(
        shards,
        mesh=mesh,
        in_specs=(P("rows", "cols", None), P(), P("rows", "cols"), P("rows", "cols"), P(), P()),
        out_specs=P("rows", "cols"),
        check_vma=False,
    )
```

```python
import jax
import jax.numpy as jnp
from jax import lax
from jax.experimental import pallas as pl
from jax.experimental.pallas import tpu as pltpu
from jax.sharding import PartitionSpec as P

D_PROJ = 128
MESH = pl.DeviceIdType.MESH
F32, BF16 = jnp.float32, jnp.bfloat16

ROWS, COLS, CHANNELS, PICKS = 32, 128, 1536, 512
SLOTS = 16
LINE_SLOTS = 64
CHUNK = 256
CHUNKS = CHANNELS // CHUNK
AHEAD = 3
BAND = 8
WIDE = COLS + 16
TABLE = (ROWS + 4) * WIDE


def padded_2(block, sides, width):
    for axis, dim in sides:
        count = lax.axis_size(axis)
        forward = [(i, i + 1) for i in range(count - 1)]
        backward = [(target, source) for source, target in forward]
        low = lax.ppermute(
            lax.slice_in_dim(block, block.shape[dim] - width, None, axis=dim), axis, forward
        )
        high = lax.ppermute(lax.slice_in_dim(block, 0, width, axis=dim), axis, backward)
        block = jnp.concatenate([low, block, high], axis=dim)
    return block


def window_sum(padded, rows_dev, cols_dev):
    total = jnp.zeros((rows_dev, cols_dev, padded.shape[2]), jnp.float32)
    for row_off in range(3):
        for col_off in range(3):
            total = total + padded[
                row_off : row_off + rows_dev, col_off : col_off + cols_dev
            ].astype(jnp.float32)
    return total / 9.0


def any_picks(features, projection, prev_dist, valid, pick_owner, pick_slot):
    rows_dev, cols_dev, channels = features.shape
    proj_full = projection.astype(jnp.float32)
    own_index = lax.axis_index("rows") * lax.axis_size("cols") + lax.axis_index("cols")
    owned = pick_owner == own_index
    padded = padded_2(features, (("rows", 0), ("cols", 1)), 1)
    pooled = window_sum(padded, rows_dev, cols_dev).reshape(rows_dev * cols_dev, channels)
    projected = jnp.dot(pooled, proj_full, precision=lax.Precision.HIGHEST)
    local_rows = jnp.where(owned[:, None], projected[pick_slot], jnp.float32(0.0))
    pick_rows = local_rows
    for axis in ("rows", "cols"):
        count, step = lax.axis_size(axis), 1
        while step < count:
            swap = [(i, i ^ step) for i in range(count)]
            pick_rows = pick_rows + lax.ppermute(pick_rows, axis, swap)
            step *= 2
    pick_sq = jnp.sum(pick_rows * pick_rows, axis=1)
    own_sq = jnp.sum(projected * projected, axis=1)
    inner_prod = jnp.dot(projected, pick_rows.T, precision=lax.Precision.HIGHEST)
    scaled_gap = (own_sq[:, None] + pick_sq[None, :] - 2.0 * inner_prod) / D_PROJ
    nearest = jnp.min(scaled_gap, axis=1).reshape(rows_dev, cols_dev)
    return jnp.where(valid == 1, jnp.minimum(prev_dist, nearest), jnp.float32(0.0))


def iota(shape, dim):
    return lax.broadcasted_iota(jnp.int32, shape, dim)


def dot(a, b):
    return jnp.dot(a, b, preferred_element_type=F32)


def touches(pick_row, pick_col, row0, col0, rows=ROWS, cols=COLS):
    down, across = pick_row - row0, pick_col - col0
    return (down >= -1) & (down <= rows) & (across >= -1) & (across <= cols)


def kernel(
    feat_hbm, proj_hbm, prev_hbm, valid_hbm, owner_hbm, slot_hbm, out_ref, most_ref,
    owner_ref, slot_ref, proj_ref, prev_ref, valid_ref,
    feat, raw, band, pooled, hrow, ends, mine, line, packed, plane, onehot,
    rhs, lhs, own_sq, best, from_up, from_down, from_left, from_right, corner, side,
    load_sem, small_sem, send_sem, recv_sem, halo_send, halo_recv,
):
    r, c = lax.axis_index("rows"), lax.axis_index("cols")
    x, core = r // 2, r % 2
    y, z = c // 8, c % 8
    up, down = lax.rem(r + 7, 8), lax.rem(r + 1, 8)
    left, right = lax.rem(c + 31, 32), lax.rem(c + 1, 32)

    def on_line(step):
        return (x * 2 + lax.rem(core + step // 8, 2), y * 8 + lax.rem(z + step % 8, 8))

    def on_plane(step):
        return (lax.rem(x + step // 4, 4) * 2 + core, lax.rem(y + step % 4, 4) * 8 + z)

    loads = [
        pltpu.make_async_copy(feat_hbm.at[:, :, pl.ds(i * CHUNK, CHUNK)], feat.at[i], load_sem.at[i])
        for i in range(CHUNKS)
    ]
    smalls = [
        pltpu.make_async_copy(source, target, small_sem.at[n])
        for n, (source, target) in enumerate(
            (
                (owner_hbm, owner_ref),
                (slot_hbm, slot_ref),
                (proj_hbm, proj_ref),
                (prev_hbm, prev_ref),
                (valid_hbm, valid_ref),
            )
        )
    ]
    for load in smalls[:3] + loads[:AHEAD] + smalls[3:]:
        load.start()

    barrier = pltpu.get_barrier_semaphore()

    def greet(device):
        pl.semaphore_signal(barrier, inc=1, device_id=device, device_id_type=MESH)

    def greet_line(step, _):
        greet(on_line(step))
        return 0

    def greet_plane(step, _):
        greet(on_plane(step))
        return 0

    lax.fori_loop(1, 16, greet_line, 0)
    lax.fori_loop(1, 16, greet_plane, 0)
    around = [(up, c), (down, c), (r, left), (r, right)]
    around += [(up, left), (up, right), (down, left), (down, right)]
    for device in around:
        greet(device)

    smalls[0].wait()
    smalls[1].wait()
    owner, slot = owner_ref[...], slot_ref[...]
    pick_row = (owner >> 5) * ROWS + (slot >> 7)
    pick_col = (owner & 31) * COLS + (slot & 127)
    here = jnp.broadcast_to(touches(pick_row, pick_col, r * ROWS, c * COLS), (SLOTS, PICKS))
    before = (iota((PICKS, PICKS), 0) < iota((PICKS, PICKS), 1)).astype(F32).astype(BF16)
    rank = dot(here.astype(F32).astype(BF16), before)
    tile_row, tile_col = pick_row - r * ROWS, pick_col - c * COLS
    place = (tile_row + 2) * WIDE + tile_col + 8
    chosen = here & (rank == iota((SLOTS, PICKS), 0).astype(F32))
    places = jnp.sum(
        jnp.where(chosen, jnp.broadcast_to(place, (SLOTS, PICKS)).astype(F32), 0.0), axis=1, keepdims=True
    ).astype(jnp.int32)
    places = jnp.clip(places, WIDE + 1, TABLE - WIDE - 2)
    filled = jnp.sum(chosen.astype(F32), axis=1, keepdims=True)

    raw[0 : 2 * WIDE] = jnp.zeros((2 * WIDE, D_PROJ), F32)
    raw[TABLE - 2 * WIDE :] = jnp.zeros((2 * WIDE, D_PROJ), F32)
    smalls[2].wait()
    proj = proj_ref[...]
    margin = jnp.zeros((8, D_PROJ), F32)
    for row in range(2, ROWS + 2):
        raw[row * WIDE : row * WIDE + 8] = margin
        raw[row * WIDE + 8 + COLS : (row + 1) * WIDE] = margin
    for i in range(CHUNKS):
        loads[i].wait()
        if i + AHEAD < CHUNKS:
            loads[i + AHEAD].start()
        for top in range(0, ROWS, BAND):
            block = feat[i, top : top + BAND].reshape(BAND * COLS, CHUNK)
            done = dot(block, proj[i * CHUNK : (i + 1) * CHUNK])
            for k in range(BAND):
                at = (top + k + 2) * WIDE + 8
                one = done[k * COLS : (k + 1) * COLS]
                raw[at : at + COLS] = one if i == 0 else raw[at : at + COLS] + one

    for j in range(SLOTS):
        place = places[j, 0]
        near = raw[pl.ds(place - WIDE - 1, 3), :] + raw[pl.ds(place - 1, 3), :]
        near += raw[pl.ds(place + WIDE - 1, 3), :]
        mine[j : j + 1] = near[0:1] + near[1:2] + near[2:3]
    mine[...] = jnp.where(filled > 0.0, mine[...], 0.0)
    spot = core * 8 + z
    line[spot] = mine[...]

    pl.semaphore_wait(barrier, 38)

    for step in (4, 12, 5, 13, 3, 11, 6, 14, 2, 10, 7, 15, 1, 9, 8):
        pltpu.make_async_remote_copy(
            mine, line.at[spot], send_sem.at[0], recv_sem.at[0],
            device_id=on_line(step), device_id_type=MESH,
        ).start()


    for n, at in enumerate((2 * WIDE, (ROWS + 1) * WIDE)):
        hrow[n] = raw[at + 7 : at + 7 + COLS] + raw[at + 8 : at + 8 + COLS] + raw[at + 9 : at + 9 + COLS]
    for n in range(2):
        first = 2 * WIDE + 8 + n * (COLS - 1)
        inner = raw[pl.ds(first, ROWS, stride=WIDE), :]
        outer = raw[pl.ds(first - WIDE, ROWS, stride=WIDE), :]
        outer += raw[pl.ds(first + WIDE, ROWS, stride=WIDE), :]
        ends[n, 0:32] = inner + outer
        ends[n, 32:40] = jnp.broadcast_to(inner[0:1], (8, D_PROJ))
        ends[n, 40:48] = jnp.broadcast_to(inner[ROWS - 1 :], (8, D_PROJ))
    halos = [
        (hrow.at[0], from_down, (up, c)),
        (hrow.at[1], from_up, (down, c)),
        (ends.at[0, pl.ds(0, 32)], from_right, (r, left)),
        (ends.at[1, pl.ds(0, 32)], from_left, (r, right)),
        (ends.at[0, pl.ds(32, 8)], corner.at[3], (up, left)),
        (ends.at[1, pl.ds(32, 8)], corner.at[2], (up, right)),
        (ends.at[0, pl.ds(40, 8)], corner.at[1], (down, left)),
        (ends.at[1, pl.ds(40, 8)], corner.at[0], (down, right)),
    ]
    halo_copies = []
    for n, (source, target, device) in enumerate(halos):
        copy = pltpu.make_async_remote_copy(
            source, target, halo_send.at[n], halo_recv.at[n], device_id=device, device_id_type=MESH
        )
        copy.start()
        halo_copies.append(copy)

    grid = jnp.concatenate(
        [jnp.broadcast_to(pick_row, (4, PICKS)), jnp.broadcast_to(pick_col, (4, PICKS))], axis=0
    ).astype(F32)
    grid = grid.T
    rows_k, cols_k = grid[:, 0:1], grid[:, 4:5]
    me = x * 4 + y
    d = iota((1, 128), 1)
    row0 = (((d >> 5) * 2) * ROWS).astype(F32)
    col0 = ((((d >> 3) & 3) * 8 + (d & 7)) * COLS).astype(F32)
    most = jnp.zeros((1, 128), F32)
    for half in range(2):
        over = touches(rows_k, cols_k, row0 + half * ROWS, col0).astype(F32)
        most = jnp.maximum(most, jnp.sum(over, axis=0, keepdims=True))
    earlier = (iota((PICKS, PICKS), 1) < iota((PICKS, PICKS), 0)).astype(F32).astype(BF16)
    row0, col0 = ((d >> 2) * (2 * ROWS)).astype(F32), ((d & 3) * (8 * COLS)).astype(F32)
    over = touches(rows_k, cols_k, row0, col0, 2 * ROWS, 8 * COLS) & (d < 16)
    in_line = jnp.sum(over.astype(F32), axis=0, keepdims=True)
    most_ref[0] = (
        (jnp.max(most) > float(SLOTS)) | (jnp.max(in_line) > float(LINE_SLOTS))
    ).astype(jnp.int32)
    ranks = dot(earlier, over.astype(F32).astype(BF16))
    ranks = jnp.where(over, jnp.minimum(ranks, 100.0), 200.0)
    spread = ((iota((128, 1024), 1) >> 6) == iota((128, 1024), 0)).astype(F32).astype(BF16)
    onehot[...] = (
        (dot(ranks.astype(BF16), spread) == (iota((PICKS, 1024), 1) & 63).astype(F32))
        .astype(F32)
        .astype(BF16)
    )
    here = jnp.sum(jnp.where(d == me, ranks, 0.0), axis=1, keepdims=True)
    goes = (here == iota((PICKS, 128), 1).astype(F32)).astype(F32).T[:LINE_SLOTS].astype(BF16)
    d = iota((1, 16 * SLOTS), 1)
    row0 = ((x * 2 + d // (8 * SLOTS)) * ROWS).astype(F32)
    col0 = ((y * 8 + (d // SLOTS) % 8) * COLS).astype(F32)
    over = touches(rows_k, cols_k, row0, col0)
    ranks = dot(earlier, over.astype(F32).astype(BF16))
    comes = (over & (ranks == (d % SLOTS).astype(F32))).astype(F32).astype(BF16)
    gather = dot(goes, comes).astype(BF16)

    def pool(i, _):
        at = pl.multiple_of(i * WIDE, 8)
        down_sum = raw[pl.ds(at + WIDE, WIDE), :] + raw[pl.ds(at + 2 * WIDE, WIDE), :]
        slot = lax.rem(i, 4)
        band[slot] = down_sum + raw[pl.ds(at + 3 * WIDE, WIDE), :]
        across = band[slot, 7 : 7 + COLS] + band[slot, 8 : 8 + COLS] + band[slot, 9 : 9 + COLS]
        pooled[pl.ds(pl.multiple_of(i * COLS, COLS), COLS), :] = across
        return 0

    lax.fori_loop(0, ROWS, pool, 0, unroll=4)

    pltpu.make_async_copy(line.at[pl.ds(0, 15)], line.at[pl.ds(0, 15)], recv_sem.at[0]).wait()
    got = line[...].reshape(16 * SLOTS, D_PROJ)
    high = got.astype(BF16)
    rest = got - high.astype(F32)
    middle = rest.astype(BF16)
    low = (rest - middle.astype(F32)).astype(BF16)
    three = dot(gather, jnp.concatenate([high, middle, low], axis=1))
    packed[...] = three[:, :D_PROJ] + three[:, D_PROJ : 2 * D_PROJ] + three[:, 2 * D_PROJ :]

    for step in (10, 6, 14, 9, 11, 2, 8, 5, 7, 13, 15, 1, 3, 4, 12):
        pltpu.make_async_remote_copy(
            packed, plane.at[me], send_sem.at[1], recv_sem.at[1],
            device_id=on_plane(step), device_id_type=MESH,
        ).start()

    plane[me] = packed[...]

    for copy in halo_copies:
        copy.wait_recv()
    has_up, has_down = (r > 0).astype(F32), (r < 7).astype(F32)
    has_left, has_right = (c > 0).astype(F32), (c < 31).astype(F32)
    side[0] = from_left[...] * has_left
    side[1] = from_right[...] * has_right
    side[0, 0:1] += corner[0, 0:1] * (has_up * has_left)
    side[1, 0:1] += corner[1, 0:1] * (has_up * has_right)
    side[0, 31:32] += corner[2, 0:1] * (has_down * has_left)
    side[1, 31:32] += corner[3, 0:1] * (has_down * has_right)
    pooled[0:COLS] += from_up[...] * has_up
    pooled[(ROWS - 1) * COLS :] += from_down[...] * has_down
    sub = iota((COLS, D_PROJ), 0)

    def lay_out(i, _):
        at = pl.multiple_of(i * COLS, COLS)
        one = pooled[pl.ds(at, COLS), :]
        one += jnp.where(sub == 0, side[0, pl.ds(i, 1), :], 0.0)
        one += jnp.where(sub == COLS - 1, side[1, pl.ds(i, 1), :], 0.0)
        flipped = one.T
        own_sq[pl.ds(i, 1), :] = jnp.sum(flipped * flipped, axis=0, keepdims=True)
        high = flipped.astype(BF16)
        low = (flipped - high.astype(F32)).astype(BF16)
        rhs[0:128, pl.ds(at, COLS)] = high
        rhs[128:256, pl.ds(at, COLS)] = low
        rhs[256:384, pl.ds(at, COLS)] = high
        return 0

    lax.fori_loop(0, ROWS, lay_out, 0, unroll=2)

    pltpu.make_async_copy(plane.at[pl.ds(0, 15)], plane.at[pl.ds(0, 15)], recv_sem.at[1]).wait()
    got = plane[...].reshape(1024, D_PROJ)
    high = got.astype(BF16)
    low = (got - high.astype(F32)).astype(BF16)
    both = dot(onehot[...], jnp.concatenate([high, low], axis=1))
    picks = both[:, :D_PROJ] + both[:, D_PROJ:]
    high = picks.astype(BF16)
    lhs[:, 0:128] = high
    lhs[:, 128:256] = high
    lhs[:, 256:384] = (picks - high.astype(F32)).astype(BF16)
    half_sq = jnp.sum(picks * picks, axis=1, keepdims=True) * 0.5
    for i in range(ROWS // 2):
        score = dot(lhs[...], rhs[:, i * 256 : (i + 1) * 256]) - half_sq
        score = jnp.max(score, axis=0, keepdims=True)
        best[2 * i : 2 * i + 1] = score[:, :128]
        best[2 * i + 1 : 2 * i + 2] = score[:, 128:]
    smalls[3].wait()
    smalls[4].wait()
    gap = (own_sq[...] - 2.0 * best[...]) * (1.0 / (81.0 * D_PROJ))
    out_ref[...] = jnp.where(valid_ref[...] == 1, jnp.minimum(prev_ref[...], gap), 0.0)

    pltpu.make_async_copy(line.at[pl.ds(0, 15)], line.at[pl.ds(0, 15)], send_sem.at[0]).wait()
    pltpu.make_async_copy(plane.at[pl.ds(0, 15)], plane.at[pl.ds(0, 15)], send_sem.at[1]).wait()
    for copy in halo_copies:
        copy.wait_send()


def shards(features, projection, prev_dist, valid, pick_owner, pick_slot):
    vmem = pl.BlockSpec(memory_space=pltpu.VMEM)
    result, most = pl.pallas_call(
        kernel,
        out_shape=(
            jax.ShapeDtypeStruct((ROWS, COLS), F32),
            jax.ShapeDtypeStruct((1,), jnp.int32),
        ),
        in_specs=[pl.BlockSpec(memory_space=pltpu.HBM)] * 6,
        out_specs=(vmem, pl.BlockSpec(memory_space=pltpu.SMEM)),
        scratch_shapes=[
            pltpu.VMEM((1, PICKS), jnp.int32),
            pltpu.VMEM((1, PICKS), jnp.int32),
            pltpu.VMEM((CHANNELS, D_PROJ), BF16),
            pltpu.VMEM((ROWS, COLS), F32),
            pltpu.VMEM((ROWS, COLS), jnp.int32),
            pltpu.VMEM((CHUNKS, ROWS, COLS, CHUNK), BF16),
            pltpu.VMEM((TABLE, D_PROJ), F32),
            pltpu.VMEM((4, WIDE, D_PROJ), F32),
            pltpu.VMEM((ROWS * COLS, D_PROJ), F32),
            pltpu.VMEM((2, COLS, D_PROJ), F32),
            pltpu.VMEM((2, 48, D_PROJ), F32),
            pltpu.VMEM((SLOTS, D_PROJ), F32),
            pltpu.VMEM((16, SLOTS, D_PROJ), F32),
            pltpu.VMEM((LINE_SLOTS, D_PROJ), F32),
            pltpu.VMEM((16, LINE_SLOTS, D_PROJ), F32),
            pltpu.VMEM((PICKS, 1024), BF16),
            pltpu.VMEM((384, ROWS * COLS), BF16),
            pltpu.VMEM((PICKS, 384), BF16),
            pltpu.VMEM((ROWS, COLS), F32),
            pltpu.VMEM((ROWS, COLS), F32),
            pltpu.VMEM((COLS, D_PROJ), F32),
            pltpu.VMEM((COLS, D_PROJ), F32),
            pltpu.VMEM((ROWS, D_PROJ), F32),
            pltpu.VMEM((ROWS, D_PROJ), F32),
            pltpu.VMEM((4, 8, D_PROJ), F32),
            pltpu.VMEM((2, ROWS, D_PROJ), F32),
            pltpu.SemaphoreType.DMA((CHUNKS,)),
            pltpu.SemaphoreType.DMA((5,)),
            pltpu.SemaphoreType.DMA((2,)),
            pltpu.SemaphoreType.DMA((2,)),
            pltpu.SemaphoreType.DMA((8,)),
            pltpu.SemaphoreType.DMA((8,)),
        ],
        compiler_params=pltpu.CompilerParams(
            collective_id=0, has_side_effects=True, vmem_limit_bytes=56 << 20
        ),
        name="coreset",
    )(
        features, projection, prev_dist, valid,
        pick_owner.reshape(1, PICKS), pick_slot.reshape(1, PICKS),
    )
    return lax.cond(
        most[0] > 0,
        any_picks,
        lambda *_: result,
        features, projection, prev_dist, valid, pick_owner, pick_slot,
    )


def solution(mesh):
    return jax.shard_map(
        shards,
        mesh=mesh,
        in_specs=(P("rows", "cols", None), P(), P("rows", "cols"), P("rows", "cols"), P(), P()),
        out_specs=P("rows", "cols"),
        check_vma=False,
    )
```

```python
import jax
import jax.numpy as jnp
from jax import lax
from jax.experimental import pallas as pl
from jax.experimental.pallas import tpu as pltpu
from jax.sharding import PartitionSpec as P

D_PROJ = 128
MESH = pl.DeviceIdType.MESH
F32, BF16 = jnp.float32, jnp.bfloat16

ROWS, COLS, CHANNELS, PICKS = 32, 128, 1536, 512
SLOTS = 16
LINE_SLOTS = 64
CHUNK = 256
CHUNKS = CHANNELS // CHUNK
AHEAD = 3
BAND = 8
WIDE = COLS + 16
TABLE = (ROWS + 4) * WIDE


def padded_2(block, sides, width):
    for axis, dim in sides:
        count = lax.axis_size(axis)
        forward = [(i, i + 1) for i in range(count - 1)]
        backward = [(target, source) for source, target in forward]
        low = lax.ppermute(
            lax.slice_in_dim(block, block.shape[dim] - width, None, axis=dim), axis, forward
        )
        high = lax.ppermute(lax.slice_in_dim(block, 0, width, axis=dim), axis, backward)
        block = jnp.concatenate([low, block, high], axis=dim)
    return block


def window_sum(padded, rows_dev, cols_dev):
    total = jnp.zeros((rows_dev, cols_dev, padded.shape[2]), jnp.float32)
    for row_off in range(3):
        for col_off in range(3):
            total = total + padded[
                row_off : row_off + rows_dev, col_off : col_off + cols_dev
            ].astype(jnp.float32)
    return total / 9.0


def any_picks(features, projection, prev_dist, valid, pick_owner, pick_slot):
    rows_dev, cols_dev, channels = features.shape
    proj_full = projection.astype(jnp.float32)
    own_index = lax.axis_index("rows") * lax.axis_size("cols") + lax.axis_index("cols")
    owned = pick_owner == own_index
    padded = padded_2(features, (("rows", 0), ("cols", 1)), 1)
    pooled = window_sum(padded, rows_dev, cols_dev).reshape(rows_dev * cols_dev, channels)
    projected = jnp.dot(pooled, proj_full, precision=lax.Precision.HIGHEST)
    local_rows = jnp.where(owned[:, None], projected[pick_slot], jnp.float32(0.0))
    pick_rows = local_rows
    for axis in ("rows", "cols"):
        count, step = lax.axis_size(axis), 1
        while step < count:
            swap = [(i, i ^ step) for i in range(count)]
            pick_rows = pick_rows + lax.ppermute(pick_rows, axis, swap)
            step *= 2
    pick_sq = jnp.sum(pick_rows * pick_rows, axis=1)
    own_sq = jnp.sum(projected * projected, axis=1)
    inner_prod = jnp.dot(projected, pick_rows.T, precision=lax.Precision.HIGHEST)
    scaled_gap = (own_sq[:, None] + pick_sq[None, :] - 2.0 * inner_prod) / D_PROJ
    nearest = jnp.min(scaled_gap, axis=1).reshape(rows_dev, cols_dev)
    return jnp.where(valid == 1, jnp.minimum(prev_dist, nearest), jnp.float32(0.0))


def iota(shape, dim):
    return lax.broadcasted_iota(jnp.int32, shape, dim)


def dot(a, b):
    return jnp.dot(a, b, preferred_element_type=F32)


def touches(pick_row, pick_col, row0, col0, rows=ROWS, cols=COLS):
    down, across = pick_row - row0, pick_col - col0
    return (down >= -1) & (down <= rows) & (across >= -1) & (across <= cols)


def kernel(
    feat_hbm, proj_hbm, prev_hbm, valid_hbm, owner_hbm, slot_hbm, out_ref, most_ref,
    owner_ref, slot_ref, proj_ref, prev_ref, valid_ref,
    feat, raw, band, pooled, hrow, ends, mine, line, packed, plane, onehot,
    rhs, lhs, own_sq, best, from_up, from_down, from_left, from_right, corner, side,
    load_sem, small_sem, send_sem, recv_sem, halo_send, halo_recv,
):
    r, c = lax.axis_index("rows"), lax.axis_index("cols")
    x, core = r // 2, r % 2
    y, z = c // 8, c % 8
    up, down = lax.rem(r + 7, 8), lax.rem(r + 1, 8)
    left, right = lax.rem(c + 31, 32), lax.rem(c + 1, 32)

    def on_line(step):
        return (x * 2 + lax.rem(core + step // 8, 2), y * 8 + lax.rem(z + step % 8, 8))

    def on_plane(step):
        return (lax.rem(x + step // 4, 4) * 2 + core, lax.rem(y + step % 4, 4) * 8 + z)

    loads = [
        pltpu.make_async_copy(feat_hbm.at[:, :, pl.ds(i * CHUNK, CHUNK)], feat.at[i], load_sem.at[i])
        for i in range(CHUNKS)
    ]
    smalls = [
        pltpu.make_async_copy(source, target, small_sem.at[n])
        for n, (source, target) in enumerate(
            (
                (owner_hbm, owner_ref),
                (slot_hbm, slot_ref),
                (proj_hbm, proj_ref),
                (prev_hbm, prev_ref),
                (valid_hbm, valid_ref),
            )
        )
    ]
    for load in smalls[:3] + loads[:AHEAD] + smalls[3:]:
        load.start()

    barrier = pltpu.get_barrier_semaphore()

    def greet(device):
        pl.semaphore_signal(barrier, inc=1, device_id=device, device_id_type=MESH)

    far_line = (4, 12, 5, 13, 3, 11, 6, 14, 2, 10, 7, 15, 1, 9, 8)
    far_plane = (10, 6, 14, 9, 11, 2, 8, 5, 7, 13, 15, 1, 3, 4, 12)
    for step in far_line:
        greet(on_line(step))
    for step in far_plane:
        greet(on_plane(step))
    around = [(up, c), (down, c), (r, left), (r, right)]
    around += [(up, left), (up, right), (down, left), (down, right)]
    for device in around:
        greet(device)

    smalls[0].wait()
    smalls[1].wait()
    owner, slot = owner_ref[...], slot_ref[...]
    pick_row = (owner >> 5) * ROWS + (slot >> 7)
    pick_col = (owner & 31) * COLS + (slot & 127)
    here = jnp.broadcast_to(touches(pick_row, pick_col, r * ROWS, c * COLS), (SLOTS, PICKS))
    before = (iota((PICKS, PICKS), 0) < iota((PICKS, PICKS), 1)).astype(F32).astype(BF16)
    rank = dot(here.astype(F32).astype(BF16), before)
    tile_row, tile_col = pick_row - r * ROWS, pick_col - c * COLS
    place = (tile_row + 2) * WIDE + tile_col + 8
    chosen = here & (rank == iota((SLOTS, PICKS), 0).astype(F32))
    places = jnp.sum(
        jnp.where(chosen, jnp.broadcast_to(place, (SLOTS, PICKS)).astype(F32), 0.0), axis=1, keepdims=True
    ).astype(jnp.int32)
    places = jnp.clip(places, WIDE + 1, TABLE - WIDE - 2)
    filled = jnp.sum(chosen.astype(F32), axis=1, keepdims=True)

    raw[0 : 2 * WIDE] = jnp.zeros((2 * WIDE, D_PROJ), F32)
    raw[TABLE - 2 * WIDE :] = jnp.zeros((2 * WIDE, D_PROJ), F32)
    smalls[2].wait()
    proj = proj_ref[...]
    margin = jnp.zeros((8, D_PROJ), F32)
    for row in range(2, ROWS + 2):
        raw[row * WIDE : row * WIDE + 8] = margin
        raw[row * WIDE + 8 + COLS : (row + 1) * WIDE] = margin
    for i in range(CHUNKS):
        loads[i].wait()
        if i + AHEAD < CHUNKS:
            loads[i + AHEAD].start()
        for top in range(0, ROWS, BAND):
            block = feat[i, top : top + BAND].reshape(BAND * COLS, CHUNK)
            done = dot(block, proj[i * CHUNK : (i + 1) * CHUNK])
            for k in range(BAND):
                at = (top + k + 2) * WIDE + 8
                one = done[k * COLS : (k + 1) * COLS]
                raw[at : at + COLS] = one if i == 0 else raw[at : at + COLS] + one

    for j in range(SLOTS):
        place = places[j, 0]
        near = raw[pl.ds(place - WIDE - 1, 3), :] + raw[pl.ds(place - 1, 3), :]
        near += raw[pl.ds(place + WIDE - 1, 3), :]
        mine[j : j + 1] = near[0:1] + near[1:2] + near[2:3]
    mine[...] = jnp.where(filled > 0.0, mine[...], 0.0)
    spot = core * 8 + z
    line[spot] = mine[...]

    pl.semaphore_wait(barrier, 38)

    for step in far_line:
        pltpu.make_async_remote_copy(
            mine, line.at[spot], send_sem.at[0], recv_sem.at[0],
            device_id=on_line(step), device_id_type=MESH,
        ).start()


    for n, at in enumerate((2 * WIDE, (ROWS + 1) * WIDE)):
        hrow[n] = raw[at + 7 : at + 7 + COLS] + raw[at + 8 : at + 8 + COLS] + raw[at + 9 : at + 9 + COLS]
    for n in range(2):
        first = 2 * WIDE + 8 + n * (COLS - 1)
        inner = raw[pl.ds(first, ROWS, stride=WIDE), :]
        outer = raw[pl.ds(first - WIDE, ROWS, stride=WIDE), :]
        outer += raw[pl.ds(first + WIDE, ROWS, stride=WIDE), :]
        ends[n, 0:32] = inner + outer
        ends[n, 32:40] = jnp.broadcast_to(inner[0:1], (8, D_PROJ))
        ends[n, 40:48] = jnp.broadcast_to(inner[ROWS - 1 :], (8, D_PROJ))
    halos = [
        (hrow.at[0], from_down, (up, c)),
        (hrow.at[1], from_up, (down, c)),
        (ends.at[0, pl.ds(0, 32)], from_right, (r, left)),
        (ends.at[1, pl.ds(0, 32)], from_left, (r, right)),
        (ends.at[0, pl.ds(32, 8)], corner.at[3], (up, left)),
        (ends.at[1, pl.ds(32, 8)], corner.at[2], (up, right)),
        (ends.at[0, pl.ds(40, 8)], corner.at[1], (down, left)),
        (ends.at[1, pl.ds(40, 8)], corner.at[0], (down, right)),
    ]
    halo_copies = []
    for n, (source, target, device) in enumerate(halos):
        copy = pltpu.make_async_remote_copy(
            source, target, halo_send.at[n], halo_recv.at[n], device_id=device, device_id_type=MESH
        )
        copy.start()
        halo_copies.append(copy)

    grid = jnp.concatenate(
        [jnp.broadcast_to(pick_row, (4, PICKS)), jnp.broadcast_to(pick_col, (4, PICKS))], axis=0
    ).astype(F32)
    grid = grid.T
    rows_k, cols_k = grid[:, 0:1], grid[:, 4:5]
    me = x * 4 + y
    d = iota((1, 128), 1)
    row0 = (((d >> 5) * 2) * ROWS).astype(F32)
    col0 = ((((d >> 3) & 3) * 8 + (d & 7)) * COLS).astype(F32)
    most = jnp.zeros((1, 128), F32)
    for half in range(2):
        over = touches(rows_k, cols_k, row0 + half * ROWS, col0).astype(F32)
        most = jnp.maximum(most, jnp.sum(over, axis=0, keepdims=True))
    earlier = (iota((PICKS, PICKS), 1) < iota((PICKS, PICKS), 0)).astype(F32).astype(BF16)
    row0, col0 = ((d >> 2) * (2 * ROWS)).astype(F32), ((d & 3) * (8 * COLS)).astype(F32)
    over = touches(rows_k, cols_k, row0, col0, 2 * ROWS, 8 * COLS) & (d < 16)
    in_line = jnp.sum(over.astype(F32), axis=0, keepdims=True)
    most_ref[0] = (
        (jnp.max(most) > float(SLOTS)) | (jnp.max(in_line) > float(LINE_SLOTS))
    ).astype(jnp.int32)
    ranks = dot(earlier, over.astype(F32).astype(BF16))
    ranks = jnp.where(over, jnp.minimum(ranks, 100.0), 200.0)
    spread = ((iota((128, 1024), 1) >> 6) == iota((128, 1024), 0)).astype(F32).astype(BF16)
    onehot[...] = (
        (dot(ranks.astype(BF16), spread) == (iota((PICKS, 1024), 1) & 63).astype(F32))
        .astype(F32)
        .astype(BF16)
    )
    here = jnp.sum(jnp.where(d == me, ranks, 0.0), axis=1, keepdims=True)
    goes = (here == iota((PICKS, 128), 1).astype(F32)).astype(F32).T[:LINE_SLOTS].astype(BF16)
    d = iota((1, 16 * SLOTS), 1)
    row0 = ((x * 2 + d // (8 * SLOTS)) * ROWS).astype(F32)
    col0 = ((y * 8 + (d // SLOTS) % 8) * COLS).astype(F32)
    over = touches(rows_k, cols_k, row0, col0)
    ranks = dot(earlier, over.astype(F32).astype(BF16))
    comes = (over & (ranks == (d % SLOTS).astype(F32))).astype(F32).astype(BF16)
    gather = dot(goes, comes).astype(BF16)

    def pool(i, _):
        at = pl.multiple_of(i * WIDE, 8)
        down_sum = raw[pl.ds(at + WIDE, WIDE), :] + raw[pl.ds(at + 2 * WIDE, WIDE), :]
        slot = lax.rem(i, 4)
        band[slot] = down_sum + raw[pl.ds(at + 3 * WIDE, WIDE), :]
        across = band[slot, 7 : 7 + COLS] + band[slot, 8 : 8 + COLS] + band[slot, 9 : 9 + COLS]
        pooled[pl.ds(pl.multiple_of(i * COLS, COLS), COLS), :] = across
        return 0

    lax.fori_loop(0, ROWS, pool, 0, unroll=4)

    pltpu.make_async_copy(line.at[pl.ds(0, 15)], line.at[pl.ds(0, 15)], recv_sem.at[0]).wait()
    got = line[...].reshape(16 * SLOTS, D_PROJ)
    high = got.astype(BF16)
    rest = got - high.astype(F32)
    middle = rest.astype(BF16)
    low = (rest - middle.astype(F32)).astype(BF16)
    three = dot(gather, jnp.concatenate([high, middle, low], axis=1))
    packed[...] = three[:, :D_PROJ] + three[:, D_PROJ : 2 * D_PROJ] + three[:, 2 * D_PROJ :]

    for step in far_plane:
        pltpu.make_async_remote_copy(
            packed, plane.at[me], send_sem.at[1], recv_sem.at[1],
            device_id=on_plane(step), device_id_type=MESH,
        ).start()

    plane[me] = packed[...]

    for copy in halo_copies:
        copy.wait_recv()
    has_up, has_down = (r > 0).astype(F32), (r < 7).astype(F32)
    has_left, has_right = (c > 0).astype(F32), (c < 31).astype(F32)
    side[0] = from_left[...] * has_left
    side[1] = from_right[...] * has_right
    side[0, 0:1] += corner[0, 0:1] * (has_up * has_left)
    side[1, 0:1] += corner[1, 0:1] * (has_up * has_right)
    side[0, 31:32] += corner[2, 0:1] * (has_down * has_left)
    side[1, 31:32] += corner[3, 0:1] * (has_down * has_right)
    pooled[0:COLS] += from_up[...] * has_up
    pooled[(ROWS - 1) * COLS :] += from_down[...] * has_down
    sub = iota((COLS, D_PROJ), 0)

    def lay_out(i, _):
        at = pl.multiple_of(i * COLS, COLS)
        one = pooled[pl.ds(at, COLS), :]
        one += jnp.where(sub == 0, side[0, pl.ds(i, 1), :], 0.0)
        one += jnp.where(sub == COLS - 1, side[1, pl.ds(i, 1), :], 0.0)
        flipped = one.T
        own_sq[pl.ds(i, 1), :] = jnp.sum(flipped * flipped, axis=0, keepdims=True)
        high = flipped.astype(BF16)
        low = (flipped - high.astype(F32)).astype(BF16)
        rhs[0:128, pl.ds(at, COLS)] = high
        rhs[128:256, pl.ds(at, COLS)] = low
        rhs[256:384, pl.ds(at, COLS)] = high
        return 0

    lax.fori_loop(0, ROWS, lay_out, 0, unroll=2)

    pltpu.make_async_copy(plane.at[pl.ds(0, 15)], plane.at[pl.ds(0, 15)], recv_sem.at[1]).wait()
    got = plane[...].reshape(1024, D_PROJ)
    high = got.astype(BF16)
    low = (got - high.astype(F32)).astype(BF16)
    both = dot(onehot[...], jnp.concatenate([high, low], axis=1))
    picks = both[:, :D_PROJ] + both[:, D_PROJ:]
    high = picks.astype(BF16)
    lhs[:, 0:128] = high
    lhs[:, 128:256] = high
    lhs[:, 256:384] = (picks - high.astype(F32)).astype(BF16)
    half_sq = jnp.sum(picks * picks, axis=1, keepdims=True) * 0.5
    for i in range(ROWS // 2):
        score = dot(lhs[...], rhs[:, i * 256 : (i + 1) * 256]) - half_sq
        score = jnp.max(score, axis=0, keepdims=True)
        best[2 * i : 2 * i + 1] = score[:, :128]
        best[2 * i + 1 : 2 * i + 2] = score[:, 128:]
    smalls[3].wait()
    smalls[4].wait()
    gap = (own_sq[...] - 2.0 * best[...]) * (1.0 / (81.0 * D_PROJ))
    out_ref[...] = jnp.where(valid_ref[...] == 1, jnp.minimum(prev_ref[...], gap), 0.0)

    pltpu.make_async_copy(line.at[pl.ds(0, 15)], line.at[pl.ds(0, 15)], send_sem.at[0]).wait()
    pltpu.make_async_copy(plane.at[pl.ds(0, 15)], plane.at[pl.ds(0, 15)], send_sem.at[1]).wait()
    for copy in halo_copies:
        copy.wait_send()


def shards(features, projection, prev_dist, valid, pick_owner, pick_slot):
    vmem = pl.BlockSpec(memory_space=pltpu.VMEM)
    result, most = pl.pallas_call(
        kernel,
        out_shape=(
            jax.ShapeDtypeStruct((ROWS, COLS), F32),
            jax.ShapeDtypeStruct((1,), jnp.int32),
        ),
        in_specs=[pl.BlockSpec(memory_space=pltpu.HBM)] * 6,
        out_specs=(vmem, pl.BlockSpec(memory_space=pltpu.SMEM)),
        scratch_shapes=[
            pltpu.VMEM((1, PICKS), jnp.int32),
            pltpu.VMEM((1, PICKS), jnp.int32),
            pltpu.VMEM((CHANNELS, D_PROJ), BF16),
            pltpu.VMEM((ROWS, COLS), F32),
            pltpu.VMEM((ROWS, COLS), jnp.int32),
            pltpu.VMEM((CHUNKS, ROWS, COLS, CHUNK), BF16),
            pltpu.VMEM((TABLE, D_PROJ), F32),
            pltpu.VMEM((4, WIDE, D_PROJ), F32),
            pltpu.VMEM((ROWS * COLS, D_PROJ), F32),
            pltpu.VMEM((2, COLS, D_PROJ), F32),
            pltpu.VMEM((2, 48, D_PROJ), F32),
            pltpu.VMEM((SLOTS, D_PROJ), F32),
            pltpu.VMEM((16, SLOTS, D_PROJ), F32),
            pltpu.VMEM((LINE_SLOTS, D_PROJ), F32),
            pltpu.VMEM((16, LINE_SLOTS, D_PROJ), F32),
            pltpu.VMEM((PICKS, 1024), BF16),
            pltpu.VMEM((384, ROWS * COLS), BF16),
            pltpu.VMEM((PICKS, 384), BF16),
            pltpu.VMEM((ROWS, COLS), F32),
            pltpu.VMEM((ROWS, COLS), F32),
            pltpu.VMEM((COLS, D_PROJ), F32),
            pltpu.VMEM((COLS, D_PROJ), F32),
            pltpu.VMEM((ROWS, D_PROJ), F32),
            pltpu.VMEM((ROWS, D_PROJ), F32),
            pltpu.VMEM((4, 8, D_PROJ), F32),
            pltpu.VMEM((2, ROWS, D_PROJ), F32),
            pltpu.SemaphoreType.DMA((CHUNKS,)),
            pltpu.SemaphoreType.DMA((5,)),
            pltpu.SemaphoreType.DMA((2,)),
            pltpu.SemaphoreType.DMA((2,)),
            pltpu.SemaphoreType.DMA((8,)),
            pltpu.SemaphoreType.DMA((8,)),
        ],
        compiler_params=pltpu.CompilerParams(
            collective_id=0, has_side_effects=True, vmem_limit_bytes=56 << 20
        ),
        name="coreset",
    )(
        features, projection, prev_dist, valid,
        pick_owner.reshape(1, PICKS), pick_slot.reshape(1, PICKS),
    )
    return lax.cond(
        most[0] > 0,
        any_picks,
        lambda *_: result,
        features, projection, prev_dist, valid, pick_owner, pick_slot,
    )


def solution(mesh):
    return jax.shard_map(
        shards,
        mesh=mesh,
        in_specs=(P("rows", "cols", None), P(), P("rows", "cols"), P("rows", "cols"), P(), P()),
        out_specs=P("rows", "cols"),
        check_vma=False,
    )
```

```python
import jax
import jax.numpy as jnp
from jax import lax
from jax.experimental import pallas as pl
from jax.experimental.pallas import tpu as pltpu
from jax.sharding import PartitionSpec as P

D_PROJ = 128
MESH = pl.DeviceIdType.MESH
F32, BF16 = jnp.float32, jnp.bfloat16

ROWS, COLS, CHANNELS, PICKS = 32, 128, 1536, 512
SLOTS = 16
LINE_SLOTS = 64
CHUNK = 256
CHUNKS = CHANNELS // CHUNK
AHEAD = 3
BAND = 8
WIDE = COLS + 16
TABLE = (ROWS + 4) * WIDE


def padded_2(block, sides, width):
    for axis, dim in sides:
        count = lax.axis_size(axis)
        forward = [(i, i + 1) for i in range(count - 1)]
        backward = [(target, source) for source, target in forward]
        low = lax.ppermute(
            lax.slice_in_dim(block, block.shape[dim] - width, None, axis=dim), axis, forward
        )
        high = lax.ppermute(lax.slice_in_dim(block, 0, width, axis=dim), axis, backward)
        block = jnp.concatenate([low, block, high], axis=dim)
    return block


def window_sum(padded, rows_dev, cols_dev):
    total = jnp.zeros((rows_dev, cols_dev, padded.shape[2]), jnp.float32)
    for row_off in range(3):
        for col_off in range(3):
            total = total + padded[
                row_off : row_off + rows_dev, col_off : col_off + cols_dev
            ].astype(jnp.float32)
    return total / 9.0


def any_picks(features, projection, prev_dist, valid, pick_owner, pick_slot):
    rows_dev, cols_dev, channels = features.shape
    proj_full = projection.astype(jnp.float32)
    own_index = lax.axis_index("rows") * lax.axis_size("cols") + lax.axis_index("cols")
    owned = pick_owner == own_index
    padded = padded_2(features, (("rows", 0), ("cols", 1)), 1)
    pooled = window_sum(padded, rows_dev, cols_dev).reshape(rows_dev * cols_dev, channels)
    projected = jnp.dot(pooled, proj_full, precision=lax.Precision.HIGHEST)
    local_rows = jnp.where(owned[:, None], projected[pick_slot], jnp.float32(0.0))
    pick_rows = local_rows
    for axis in ("rows", "cols"):
        count, step = lax.axis_size(axis), 1
        while step < count:
            swap = [(i, i ^ step) for i in range(count)]
            pick_rows = pick_rows + lax.ppermute(pick_rows, axis, swap)
            step *= 2
    pick_sq = jnp.sum(pick_rows * pick_rows, axis=1)
    own_sq = jnp.sum(projected * projected, axis=1)
    inner_prod = jnp.dot(projected, pick_rows.T, precision=lax.Precision.HIGHEST)
    scaled_gap = (own_sq[:, None] + pick_sq[None, :] - 2.0 * inner_prod) / D_PROJ
    nearest = jnp.min(scaled_gap, axis=1).reshape(rows_dev, cols_dev)
    return jnp.where(valid == 1, jnp.minimum(prev_dist, nearest), jnp.float32(0.0))


def iota(shape, dim):
    return lax.broadcasted_iota(jnp.int32, shape, dim)


def dot(a, b):
    return jnp.dot(a, b, preferred_element_type=F32)


def touches(pick_row, pick_col, row0, col0, rows=ROWS, cols=COLS):
    down, across = pick_row - row0, pick_col - col0
    return (down >= -1) & (down <= rows) & (across >= -1) & (across <= cols)


def kernel(
    feat_hbm, proj_hbm, prev_hbm, valid_hbm, owner_hbm, slot_hbm, out_ref, most_ref,
    owner_ref, slot_ref, proj_ref, prev_ref, valid_ref,
    feat, raw, band, pooled, hrow, ends, mine, line, packed, plane, onehot,
    rhs, lhs, own_sq, best, from_up, from_down, from_left, from_right, corner, side,
    load_sem, small_sem, send_sem, recv_sem, halo_send, halo_recv,
):
    r, c = lax.axis_index("rows"), lax.axis_index("cols")
    x, core = r // 2, r % 2
    y, z = c // 8, c % 8
    up, down = lax.rem(r + 7, 8), lax.rem(r + 1, 8)
    left, right = lax.rem(c + 31, 32), lax.rem(c + 1, 32)

    def on_line(step):
        return (x * 2 + lax.rem(core + step // 8, 2), y * 8 + lax.rem(z + step % 8, 8))

    def on_plane(step):
        return (lax.rem(x + step // 4, 4) * 2 + core, lax.rem(y + step % 4, 4) * 8 + z)

    loads = [
        pltpu.make_async_copy(feat_hbm.at[:, :, pl.ds(i * CHUNK, CHUNK)], feat.at[i], load_sem.at[i])
        for i in range(CHUNKS)
    ]
    smalls = [
        pltpu.make_async_copy(source, target, small_sem.at[n])
        for n, (source, target) in enumerate(
            (
                (owner_hbm, owner_ref),
                (slot_hbm, slot_ref),
                (proj_hbm, proj_ref),
                (prev_hbm, prev_ref),
                (valid_hbm, valid_ref),
            )
        )
    ]
    for load in smalls[:3] + loads[:AHEAD] + smalls[3:]:
        load.start()

    barrier = pltpu.get_barrier_semaphore()

    def greet(device):
        pl.semaphore_signal(barrier, inc=1, device_id=device, device_id_type=MESH)

    far_line = (4, 12, 5, 13, 3, 11, 6, 14, 2, 10, 7, 15, 1, 9, 8)
    far_plane = (10, 6, 14, 9, 11, 2, 8, 5, 7, 13, 15, 1, 3, 4, 12)
    for step in far_line:
        greet(on_line(step))
    for step in far_plane:
        greet(on_plane(step))
    around = [(up, c), (down, c), (r, left), (r, right)]
    around += [(up, left), (up, right), (down, left), (down, right)]
    for device in around:
        greet(device)

    smalls[0].wait()
    smalls[1].wait()
    owner, slot = owner_ref[...], slot_ref[...]
    pick_row = (owner >> 5) * ROWS + (slot >> 7)
    pick_col = (owner & 31) * COLS + (slot & 127)
    here = jnp.broadcast_to(touches(pick_row, pick_col, r * ROWS, c * COLS), (SLOTS, PICKS))
    before = (iota((PICKS, PICKS), 0) < iota((PICKS, PICKS), 1)).astype(F32).astype(BF16)
    rank = dot(here.astype(F32).astype(BF16), before)
    tile_row, tile_col = pick_row - r * ROWS, pick_col - c * COLS
    place = (tile_row + 2) * WIDE + tile_col + 8
    chosen = here & (rank == iota((SLOTS, PICKS), 0).astype(F32))
    places = jnp.sum(
        jnp.where(chosen, jnp.broadcast_to(place, (SLOTS, PICKS)).astype(F32), 0.0), axis=1, keepdims=True
    ).astype(jnp.int32)
    places = jnp.clip(places, WIDE + 1, TABLE - WIDE - 2)
    filled = jnp.sum(chosen.astype(F32), axis=1, keepdims=True)

    raw[0 : 2 * WIDE] = jnp.zeros((2 * WIDE, D_PROJ), F32)
    raw[TABLE - 2 * WIDE :] = jnp.zeros((2 * WIDE, D_PROJ), F32)
    smalls[2].wait()
    proj = proj_ref[...]
    margin = jnp.zeros((8, D_PROJ), F32)
    for row in range(2, ROWS + 2):
        raw[row * WIDE : row * WIDE + 8] = margin
        raw[row * WIDE + 8 + COLS : (row + 1) * WIDE] = margin
    for i in range(CHUNKS):
        loads[i].wait()
        if i + AHEAD < CHUNKS:
            loads[i + AHEAD].start()
        for top in range(0, ROWS, BAND):
            block = feat[i, top : top + BAND].reshape(BAND * COLS, CHUNK)
            done = dot(block, proj[i * CHUNK : (i + 1) * CHUNK])
            for k in range(BAND):
                at = (top + k + 2) * WIDE + 8
                one = done[k * COLS : (k + 1) * COLS]
                raw[at : at + COLS] = one if i == 0 else raw[at : at + COLS] + one

    for j in range(SLOTS):
        place = places[j, 0]
        near = raw[pl.ds(place - WIDE - 1, 3), :] + raw[pl.ds(place - 1, 3), :]
        near += raw[pl.ds(place + WIDE - 1, 3), :]
        mine[j : j + 1] = near[0:1] + near[1:2] + near[2:3]
    mine[...] = jnp.where(filled > 0.0, mine[...], 0.0)
    spot = core * 8 + z
    line[spot] = mine[...]

    pl.semaphore_wait(barrier, 38)

    for step in far_line:
        pltpu.make_async_remote_copy(
            mine, line.at[spot], send_sem.at[0], recv_sem.at[0],
            device_id=on_line(step), device_id_type=MESH,
        ).start()


    for n, at in enumerate((2 * WIDE, (ROWS + 1) * WIDE)):
        hrow[n] = raw[at + 7 : at + 7 + COLS] + raw[at + 8 : at + 8 + COLS] + raw[at + 9 : at + 9 + COLS]
    for n in range(2):
        first = 2 * WIDE + 8 + n * (COLS - 1)
        inner = raw[pl.ds(first, ROWS, stride=WIDE), :]
        outer = raw[pl.ds(first - WIDE, ROWS, stride=WIDE), :]
        outer += raw[pl.ds(first + WIDE, ROWS, stride=WIDE), :]
        ends[n, 0:32] = inner + outer
        ends[n, 32:40] = jnp.broadcast_to(inner[0:1], (8, D_PROJ))
        ends[n, 40:48] = jnp.broadcast_to(inner[ROWS - 1 :], (8, D_PROJ))
    halos = [
        (hrow.at[0], from_down, (up, c)),
        (hrow.at[1], from_up, (down, c)),
        (ends.at[0, pl.ds(0, 32)], from_right, (r, left)),
        (ends.at[1, pl.ds(0, 32)], from_left, (r, right)),
        (ends.at[0, pl.ds(32, 8)], corner.at[3], (up, left)),
        (ends.at[1, pl.ds(32, 8)], corner.at[2], (up, right)),
        (ends.at[0, pl.ds(40, 8)], corner.at[1], (down, left)),
        (ends.at[1, pl.ds(40, 8)], corner.at[0], (down, right)),
    ]
    halo_copies = []
    for n, (source, target, device) in enumerate(halos):
        copy = pltpu.make_async_remote_copy(
            source, target, halo_send.at[n], halo_recv.at[n], device_id=device, device_id_type=MESH
        )
        copy.start()
        halo_copies.append(copy)

    grid = jnp.concatenate(
        [jnp.broadcast_to(pick_row, (4, PICKS)), jnp.broadcast_to(pick_col, (4, PICKS))], axis=0
    ).astype(F32)
    grid = grid.T
    rows_k, cols_k = grid[:, 0:1], grid[:, 4:5]
    me = x * 4 + y
    d = iota((1, 128), 1)
    row0 = (((d >> 5) * 2) * ROWS).astype(F32)
    col0 = ((((d >> 3) & 3) * 8 + (d & 7)) * COLS).astype(F32)
    most = jnp.zeros((1, 128), F32)
    for half in range(2):
        over = touches(rows_k, cols_k, row0 + half * ROWS, col0).astype(F32)
        most = jnp.maximum(most, jnp.sum(over, axis=0, keepdims=True))
    earlier = (iota((PICKS, PICKS), 1) < iota((PICKS, PICKS), 0)).astype(F32).astype(BF16)
    row0, col0 = ((d >> 2) * (2 * ROWS)).astype(F32), ((d & 3) * (8 * COLS)).astype(F32)
    over = touches(rows_k, cols_k, row0, col0, 2 * ROWS, 8 * COLS) & (d < 16)
    in_line = jnp.sum(over.astype(F32), axis=0, keepdims=True)
    most_ref[0] = (
        (jnp.max(most) > float(SLOTS)) | (jnp.max(in_line) > float(LINE_SLOTS))
    ).astype(jnp.int32)
    ranks = dot(earlier, over.astype(F32).astype(BF16))
    ranks = jnp.where(over, jnp.minimum(ranks, 100.0), 200.0)
    spread = ((iota((128, 1024), 1) >> 6) == iota((128, 1024), 0)).astype(F32).astype(BF16)
    onehot[...] = (
        (dot(ranks.astype(BF16), spread) == (iota((PICKS, 1024), 1) & 63).astype(F32))
        .astype(F32)
        .astype(BF16)
    )
    here = jnp.sum(jnp.where(d == me, ranks, 0.0), axis=1, keepdims=True)
    goes = (here == iota((PICKS, 128), 1).astype(F32)).astype(F32).T[:LINE_SLOTS].astype(BF16)
    d = iota((1, 16 * SLOTS), 1)
    row0 = ((x * 2 + d // (8 * SLOTS)) * ROWS).astype(F32)
    col0 = ((y * 8 + (d // SLOTS) % 8) * COLS).astype(F32)
    over = touches(rows_k, cols_k, row0, col0)
    ranks = dot(earlier, over.astype(F32).astype(BF16))
    comes = (over & (ranks == (d % SLOTS).astype(F32))).astype(F32).astype(BF16)
    gather = dot(goes, comes).astype(BF16)

    def pool(i, _):
        at = pl.multiple_of(i * WIDE, 8)
        down_sum = raw[pl.ds(at + WIDE, WIDE), :] + raw[pl.ds(at + 2 * WIDE, WIDE), :]
        slot = lax.rem(i, 4)
        band[slot] = down_sum + raw[pl.ds(at + 3 * WIDE, WIDE), :]
        across = band[slot, 7 : 7 + COLS] + band[slot, 8 : 8 + COLS] + band[slot, 9 : 9 + COLS]
        pooled[pl.ds(pl.multiple_of(i * COLS, COLS), COLS), :] = across
        return 0

    lax.fori_loop(0, ROWS, pool, 0, unroll=4)

    pltpu.make_async_copy(line.at[pl.ds(0, 15)], line.at[pl.ds(0, 15)], recv_sem.at[0]).wait()
    got = line[...].reshape(16 * SLOTS, D_PROJ)
    high = got.astype(BF16)
    rest = got - high.astype(F32)
    middle = rest.astype(BF16)
    low = (rest - middle.astype(F32)).astype(BF16)
    three = dot(gather, jnp.concatenate([high, middle, low], axis=1))
    packed[...] = three[:, :D_PROJ] + three[:, D_PROJ : 2 * D_PROJ] + three[:, 2 * D_PROJ :]

    for step in far_plane:
        pltpu.make_async_remote_copy(
            packed, plane.at[me], send_sem.at[1], recv_sem.at[1],
            device_id=on_plane(step), device_id_type=MESH,
        ).start()

    plane[me] = packed[...]

    for copy in halo_copies:
        copy.wait_recv()
    has_up, has_down = (r > 0).astype(F32), (r < 7).astype(F32)
    has_left, has_right = (c > 0).astype(F32), (c < 31).astype(F32)
    side[0] = from_left[...] * has_left
    side[1] = from_right[...] * has_right
    side[0, 0:1] += corner[0, 0:1] * (has_up * has_left)
    side[1, 0:1] += corner[1, 0:1] * (has_up * has_right)
    side[0, 31:32] += corner[2, 0:1] * (has_down * has_left)
    side[1, 31:32] += corner[3, 0:1] * (has_down * has_right)
    pooled[0:COLS] += from_up[...] * has_up
    pooled[(ROWS - 1) * COLS :] += from_down[...] * has_down
    sub = iota((COLS, D_PROJ), 0)

    def lay_out(i, _):
        at = pl.multiple_of(i * COLS, COLS)
        one = pooled[pl.ds(at, COLS), :]
        one += jnp.where(sub == 0, side[0, pl.ds(i, 1), :], 0.0)
        one += jnp.where(sub == COLS - 1, side[1, pl.ds(i, 1), :], 0.0)
        flipped = one.T
        own_sq[pl.ds(i, 1), :] = jnp.sum(flipped * flipped, axis=0, keepdims=True)
        high = one.astype(BF16)
        rhs[pl.ds(at, COLS), 0:128] = high
        rhs[pl.ds(at, COLS), 128:256] = (one - high.astype(F32)).astype(BF16)
        rhs[pl.ds(at, COLS), 256:384] = high
        return 0

    lax.fori_loop(0, ROWS, lay_out, 0, unroll=2)

    pltpu.make_async_copy(plane.at[pl.ds(0, 15)], plane.at[pl.ds(0, 15)], recv_sem.at[1]).wait()
    got = plane[...].reshape(1024, D_PROJ)
    high = got.astype(BF16)
    low = (got - high.astype(F32)).astype(BF16)
    both = dot(onehot[...], jnp.concatenate([high, low], axis=1))
    picks = (both[:, :D_PROJ] + both[:, D_PROJ:]).T
    high = picks.astype(BF16)
    lhs[0:128] = high
    lhs[128:256] = high
    lhs[256:384] = (picks - high.astype(F32)).astype(BF16)
    half_sq = jnp.sum(picks * picks, axis=0, keepdims=True) * 0.5

    for i in range(0, ROWS, 8):
        score = dot(rhs[i * COLS : (i + 8) * COLS], lhs[...]) - half_sq
        top = jnp.maximum(
            jnp.maximum(score[:, 0:128], score[:, 128:256]),
            jnp.maximum(score[:, 256:384], score[:, 384:512]),
        )
        for k in range(8):
            best[i + k : i + k + 1] = jnp.max(
                top[k * COLS : (k + 1) * COLS].T, axis=0, keepdims=True
            )
    smalls[3].wait()
    smalls[4].wait()
    gap = (own_sq[...] - 2.0 * best[...]) * (1.0 / (81.0 * D_PROJ))
    out_ref[...] = jnp.where(valid_ref[...] == 1, jnp.minimum(prev_ref[...], gap), 0.0)

    pltpu.make_async_copy(line.at[pl.ds(0, 15)], line.at[pl.ds(0, 15)], send_sem.at[0]).wait()
    pltpu.make_async_copy(plane.at[pl.ds(0, 15)], plane.at[pl.ds(0, 15)], send_sem.at[1]).wait()
    for copy in halo_copies:
        copy.wait_send()


def shards(features, projection, prev_dist, valid, pick_owner, pick_slot):
    vmem = pl.BlockSpec(memory_space=pltpu.VMEM)
    result, most = pl.pallas_call(
        kernel,
        out_shape=(
            jax.ShapeDtypeStruct((ROWS, COLS), F32),
            jax.ShapeDtypeStruct((1,), jnp.int32),
        ),
        in_specs=[pl.BlockSpec(memory_space=pltpu.HBM)] * 6,
        out_specs=(vmem, pl.BlockSpec(memory_space=pltpu.SMEM)),
        scratch_shapes=[
            pltpu.VMEM((1, PICKS), jnp.int32),
            pltpu.VMEM((1, PICKS), jnp.int32),
            pltpu.VMEM((CHANNELS, D_PROJ), BF16),
            pltpu.VMEM((ROWS, COLS), F32),
            pltpu.VMEM((ROWS, COLS), jnp.int32),
            pltpu.VMEM((CHUNKS, ROWS, COLS, CHUNK), BF16),
            pltpu.VMEM((TABLE, D_PROJ), F32),
            pltpu.VMEM((4, WIDE, D_PROJ), F32),
            pltpu.VMEM((ROWS * COLS, D_PROJ), F32),
            pltpu.VMEM((2, COLS, D_PROJ), F32),
            pltpu.VMEM((2, 48, D_PROJ), F32),
            pltpu.VMEM((SLOTS, D_PROJ), F32),
            pltpu.VMEM((16, SLOTS, D_PROJ), F32),
            pltpu.VMEM((LINE_SLOTS, D_PROJ), F32),
            pltpu.VMEM((16, LINE_SLOTS, D_PROJ), F32),
            pltpu.VMEM((PICKS, 1024), BF16),
            pltpu.VMEM((ROWS * COLS, 384), BF16),
            pltpu.VMEM((384, PICKS), BF16),
            pltpu.VMEM((ROWS, COLS), F32),
            pltpu.VMEM((ROWS, COLS), F32),
            pltpu.VMEM((COLS, D_PROJ), F32),
            pltpu.VMEM((COLS, D_PROJ), F32),
            pltpu.VMEM((ROWS, D_PROJ), F32),
            pltpu.VMEM((ROWS, D_PROJ), F32),
            pltpu.VMEM((4, 8, D_PROJ), F32),
            pltpu.VMEM((2, ROWS, D_PROJ), F32),
            pltpu.SemaphoreType.DMA((CHUNKS,)),
            pltpu.SemaphoreType.DMA((5,)),
            pltpu.SemaphoreType.DMA((2,)),
            pltpu.SemaphoreType.DMA((2,)),
            pltpu.SemaphoreType.DMA((8,)),
            pltpu.SemaphoreType.DMA((8,)),
        ],
        compiler_params=pltpu.CompilerParams(
            collective_id=0, has_side_effects=True, vmem_limit_bytes=56 << 20
        ),
        name="coreset",
    )(
        features, projection, prev_dist, valid,
        pick_owner.reshape(1, PICKS), pick_slot.reshape(1, PICKS),
    )
    return lax.cond(
        most[0] > 0,
        any_picks,
        lambda *_: result,
        features, projection, prev_dist, valid, pick_owner, pick_slot,
    )


def solution(mesh):
    return jax.shard_map(
        shards,
        mesh=mesh,
        in_specs=(P("rows", "cols", None), P(), P("rows", "cols"), P("rows", "cols"), P(), P()),
        out_specs=P("rows", "cols"),
        check_vma=False,
    )
```
